128 devices in a mesh: brick: 8 (over x, core), dom: 16 (over z, y).
Axes of the slice: x: 4, y: 4, z: 4, core: 2. Of those that a mesh axis runs over, the one named last changes fastest.
Arguments:
- velocity: bfloat16 [3, 27, 131072], P(None, None, ('brick', 'dom')), may hold values from -6 to 6
- adjoint: bfloat16 [3, 27, 131072], P(None, None, ('brick', 'dom')), may hold values from -6 to 6
- coupling: bfloat16 [27, 27], replicated, may hold values from -1.25 to 1.25
- jac_weight: float32 [131072], P(('brick', 'dom')), may hold values from 0.25 to 4
- owner: int32 [131072, 1], P(('brick', 'dom')), may hold values from 0 to 127; in each aligned block of 1024 rows (0 to 1023, 1024 to 2047, ...) at most 16 rows name the same one
- local_block: int32 [131072], P(('brick', 'dom')), may hold values from 0 to 4095
- offsets: int32 [128, 131072], P(None, ('brick', 'dom')), may hold values from 0 to 127
- margin: float32 [128, 131072], P(None, ('brick', 'dom')), may hold values from 0.002 to 0.02
- filtered: float32 [512, 1024, 128], P('brick', 'dom'), may hold values from 0 to 1
Outputs:
- sensitivity: float32 [512, 1024, 128], P('brick', 'dom')
- elem_density: float32 [131072], P(('brick', 'dom'))
The draws below stay inside these ranges and needn't reach their ends.
Inputs may be any that keep to these rules, and one draw needn't show every extreme that they name: Among the 1024 elements of one device at most 16 have the same owner, and exactly 16 for some owner.
All inputs are finite; a program needn't handle non-finite values.
Results may differ from the reference program's by a relative error of at most 0.0003.
Values sent between devices are 32-bit elements; how exact they have to be, the bound alone decides.
A program may use at most 64 MiB of HBM per device.

```python
import math
import jax
import jax.numpy as jnp
import numpy as np
from jax import lax

BX = 64
BY = 64
GZ = 128
ELEM_DEV = 1024
SLOTS = 128
NDEV = 128
CAP = 16
NE = 131072
GX = 512
GY = 1024
N_DOM = 16


def plant(array, key, low, largest):
    shape = array.shape
    index_at = [jax.random.randint(jax.random.fold_in(key, axis), (), 0, shape[axis]) for axis in range(len(shape))]
    array = array.at[tuple(index_at)].set(low)
    longest = shape.index(max(shape))
    index_at[longest] = (index_at[longest] + 1) % shape[longest]
    return array.at[tuple(index_at)].set(largest)


def shard_levels(key, dims, split, least, high):
    loudness, own = 1.0, jax.random.fold_in(key, 6)
    for axis_at, shards_of in split:
        steps = jnp.exp(jax.random.uniform(jax.random.fold_in(own, axis_at), (shards_of,), jnp.float32, least / len(split), high / len(split)))
        loudness = loudness * jnp.repeat(steps, dims[axis_at] // shards_of).reshape([-1 if axis == axis_at else 1 for axis in range(len(dims))])
    return loudness


def routed_block(key, own, number, rows, number_of, top, reach, lean):
    sequence = jax.random.permutation(key, number_of)
    crowded, common = load_shares(number_of, rows * top, reach, lean, True), load_shares(number_of, rows * top, reach, lean, False)
    places = jnp.arange(number_of)

    def named(sizes, turn):
        used = int((sizes > 0).sum())
        fixed = max(1, used // 4)
        moved = fixed + (places - fixed + turn * (used - fixed)) % max(1, number_of - fixed)
        return jnp.zeros((number_of,), jnp.int32).at[sequence[jnp.where(places < fixed, places, moved)]].set(jnp.asarray(sizes, jnp.int32))

    sizes = jnp.where(number % 4 == 0, named(crowded, number // 4), named(common, number - number // 4 - 1))
    mixed = jax.random.permutation(jax.random.fold_in(own, 3), number_of)
    source_of, sink = mixed[0:number_of // 2 * 2:2], mixed[1:number_of // 2 * 2:2]
    room = jnp.minimum(sizes[source_of] - 1, reach - sizes[sink]) // 2
    room = jnp.where((source_of == sequence[0]) | (sink == sequence[0]) | (sizes[sink] == 0), 0, jnp.maximum(room, 0))
    moved = jax.random.randint(jax.random.fold_in(own, 4), (number_of // 2,), 0, 1 << 20) % (room + 1)
    sizes = sizes.at[source_of].add(-moved).at[sink].add(moved)
    members = jnp.searchsorted(jnp.cumsum(sizes), jnp.arange(rows * top), side="right").astype(jnp.int32)
    table = members.reshape(top, rows).T
    table = table[jax.random.permutation(jax.random.fold_in(own, 1), rows)]
    turn = jax.random.randint(jax.random.fold_in(own, 2), (rows, 1), 0, top)
    return jnp.take_along_axis(table, (jnp.arange(top)[None, :] + turn) % top, axis=1)


def load_shares(number_of, total, reach, lean, full):
    loads = [(1 << 20) // math.isqrt(standing ** lean) + 1 for standing in range(1, number_of + 1)]
    largest = reach if full else min(reach, max(-(-total // number_of), total * loads[0] // sum(loads)))
    least = 1 if total - largest >= number_of - 1 else 0
    holding, rest = [largest] + [least] * (number_of - 1), total - largest - least * (number_of - 1)
    while rest > 0:
        movable = [i for i in range(1, number_of) if holding[i] < largest] or [i for i in range(1, number_of) if holding[i] < reach]
        whole, remaining = sum([loads[i] for i in movable]), rest
        for i in movable:
            addition = min(reach - holding[i], max(1, remaining * loads[i] // whole), rest)
            holding[i] = holding[i] + addition
            rest = rest - addition
    return np.array(holding)


def centred(key, extent, spread, most, cuts=(), held_as=jnp.bfloat16):
    factor_of = shard_levels(key, extent, cuts, -0.22, 0.18) if cuts else 1.0
    values = jax.random.normal(key, extent, jnp.float32) * spread * factor_of
    return jnp.minimum(jnp.maximum(values, -most), most).astype(held_as)


def setup_inputs(seed: int = 0) -> dict:
    streams_of = jax.random.split(jax.random.key(seed), 10)
    velocity = centred(streams_of[0], (3, 27, NE), 1.0, 6.0, ((2, 128),))
    adjoint = centred(streams_of[1], (3, 27, NE), 1.0, 6.0, ((2, 128),))
    coupling = centred(streams_of[2], (27, 27), 27 ** -0.5, 1.25)
    jac_weight = jnp.clip(jnp.exp(math.log(4.0) - 2.7725887 * jax.random.uniform(streams_of[3], (NE,), jnp.float32) ** shard_levels(streams_of[3], (NE,), ((0, 128),), -0.2, 0.2)), 0.25, 4.0)
    owner_keys = jax.random.split(jax.random.fold_in(streams_of[4], 1), NE // ELEM_DEV)
    owner_turns = jax.random.permutation(jax.random.fold_in(streams_of[4], 3), NE // ELEM_DEV)
    owner = jax.vmap(lambda own, number: routed_block(jax.random.fold_in(streams_of[4], 2), own, number, ELEM_DEV, NDEV, 1, CAP, 2))(owner_keys, owner_turns).reshape((NE, 1))
    local_block = plant(jax.random.randint(streams_of[5], (NE,), 0, BX * BY), jax.random.fold_in(streams_of[5], 1), 0, (BX * BY) - 1).astype(jnp.int32)
    offsets = plant(jax.random.randint(streams_of[6], (SLOTS, NE), 0, GZ), jax.random.fold_in(streams_of[6], 1), 0, GZ - 1).astype(jnp.int32)
    margin = jnp.clip(jnp.exp(math.log(0.02) - 2.30258502 * jax.random.uniform(streams_of[7], (SLOTS, NE), jnp.float32) ** shard_levels(streams_of[7], (SLOTS, NE), ((1, 128),), -0.2, 0.2)), 0.002, 0.02)
    filtered = jnp.clip(1.0 * jax.random.uniform(streams_of[8], (GX, GY, GZ), jnp.float32) ** shard_levels(streams_of[8], (GX, GY, GZ), ((0, 8), (1, 16)), -0.2, 0.2), 0.0, 1.0)
    return {"velocity": velocity, "adjoint": adjoint, "coupling": coupling, "jac_weight": jac_weight, "owner": owner, "local_block": local_block, "offsets": offsets, "margin": margin, "filtered": filtered}


sharpness = 8.0
threshold = 0.5
ramp_q = 0.1
radius_sq = 1.5
relax = 0.9


def project(field):
    base = jnp.tanh(sharpness * threshold)
    return (base + jnp.tanh(sharpness * (field - threshold))) / (base + jnp.tanh(sharpness * (1.0 - threshold)))


def projection_slope(field):
    base = jnp.tanh(sharpness * threshold)
    tangent = jnp.tanh(sharpness * (field - threshold))
    return sharpness * (1.0 - tangent * tangent) / (base + jnp.tanh(sharpness * (1.0 - threshold)))


def ramp_slope(density):
    return -ramp_q * (1.0 + ramp_q) / ((ramp_q + density) * (ramp_q + density))


def jacobi_sweep(field, source):
    padded = jnp.pad(field, 1)
    near = padded[2:, 1:-1, 1:-1] + padded[:-2, 1:-1, 1:-1]
    near = near + padded[1:-1, 2:, 1:-1] + padded[1:-1, :-2, 1:-1]
    near = near + padded[1:-1, 1:-1, 2:] + padded[1:-1, 1:-1, :-2]
    center = 1.0 + 6.0 * radius_sq
    return field + relax * (source - (center * field - radius_sq * near)) / center


def reference(velocity, adjoint, coupling, jac_weight, owner, local_block, offsets, margin, filtered):
    voxel_rows = project(filtered).reshape(GX * GY, GZ)
    mixed = jnp.einsum("ij,cje->cie", coupling.astype(jnp.float32), adjoint.astype(jnp.float32))
    products = jac_weight * jnp.sum(velocity.astype(jnp.float32) * mixed, axis=(0, 1))
    target = owner[:, 0]
    grid_x = (target // N_DOM) * BX + local_block // BY
    grid_y = (target % N_DOM) * BY + local_block % BY
    global_block = (grid_x * GY + grid_y).astype(jnp.int32)
    lanes = jnp.arange(GZ, dtype=jnp.int32)

    def partition(total, index):
        start = index * ELEM_DEV
        part_offsets = lax.dynamic_slice_in_dim(offsets, start, ELEM_DEV, 1)
        part_margin = lax.dynamic_slice_in_dim(margin, start, ELEM_DEV, 1)
        hits = part_offsets[:, :, None] == lanes[None, None, :]
        weights = jnp.sum(jnp.where(hits, part_margin[:, :, None], jnp.float32(0.0)), axis=0)
        blocks = lax.dynamic_slice_in_dim(global_block, start, ELEM_DEV, 0)
        density = jnp.sum(weights * voxel_rows[blocks], axis=1)
        terms = ramp_slope(density) * lax.dynamic_slice_in_dim(products, start, ELEM_DEV, 0)
        total = total.at[blocks].add(terms[:, None] * weights)
        return total, density

    total, density = lax.scan(partition, jnp.zeros((GX * GY, GZ), jnp.float32), jnp.arange(NDEV, dtype=jnp.int32))
    source = total.reshape(GX, GY, GZ) * projection_slope(filtered)
    first = jacobi_sweep(source, source)
    result = jacobi_sweep(first, source)
    return result, density.reshape(NE)
```

```python
import functools
import math

import jax
import jax.numpy as jnp
from jax import lax
from jax.experimental import pallas as pl
from jax.experimental.pallas import tpu as pltpu
from jax.sharding import PartitionSpec as P

MESH = pl.DeviceIdType.MESH
CAP = 16
LANES = 128
SHARP = 8.0
THRESHOLD = 0.5
T0 = math.tanh(SHARP * THRESHOLD)
RAMP = 0.1
F32 = jnp.float32
BF16 = jnp.bfloat16
YO = 8
NT = (((1,), (1,)), ((), ()))
NN = (((1,), (0,)), ((), ()))


def mm(a, b, dims=NN):
    return lax.dot_general(a, b, dims, preferred_element_type=F32)


def iota(shape, dim):
    return lax.broadcasted_iota(jnp.int32, shape, dim)


def onehot(mask):
    return jnp.where(mask, 1.0, 0.0).astype(F32)


def split2(x):
    hi = x.astype(BF16)
    return hi, (x - hi.astype(F32)).astype(BF16)


def split3(x):
    hi = x.astype(BF16)
    rest = x - hi.astype(F32)
    mid = rest.astype(BF16)
    return hi, mid, (rest - mid.astype(F32)).astype(BF16)


def kernel(
    nb, nd, wx, wy, coup, jac, own, loc, vel_h, adj_h, off_h, mar_h, fil_h,
    res_h, den,
    vel, adj, off, mar, th, mt, pos, wt, msend, mrecv, send, recv, ids_v, ids_s, plane,
    rows, acc, dsend, drecv, ext, fst, out,
    in_sem, smem_sem, msem, mrsem, ssem, rsem, dsem, drsem, hsem, hrsem, osem,
):
    ndev = nb * nd
    count = own.shape[1]
    blocks = count // LANES
    voxel_rows = wx * wy
    slots = ndev * CAP
    gsrc = 16
    grows = gsrc * CAP
    groups = ndev // gsrc
    brick = lax.axis_index("brick")
    dom = lax.axis_index("dom")
    me = brick * nd + dom

    def dev(lin):
        return (lin // nd, lin % nd)

    loads = [
        pltpu.make_async_copy(h, v, in_sem.at[i])
        for i, (h, v) in enumerate(((vel_h, vel), (adj_h, adj), (off_h, off), (mar_h, mar), (fil_h, th)))
    ]
    for load in loads:
        load.start()

    barrier = pltpu.get_barrier_semaphore()

    @pl.loop(1, ndev)
    def _(i):
        pl.semaphore_signal(
            barrier, inc=1, device_id=dev((me + (ndev - i)) % ndev), device_id_type=MESH
        )

    rel = (own[...] - me + ndev) % ndev
    rr = iota((LANES, 2 * LANES), 0)
    cc = iota((LANES, 2 * LANES), 1)
    upper = onehot((rr < cc) | (cc >= LANES)).astype(BF16)
    base = jnp.zeros((ndev, LANES), F32)
    for b in range(blocks):
        sl = slice(b * LANES, (b + 1) * LANES)
        hit = onehot(rel[:, sl] == iota((ndev, LANES), 0))
        hitb = hit.astype(BF16)
        mt[:, sl] = hitb
        counted = mm(hitb, upper)
        pos[:, sl] = jnp.sum((counted[:, :LANES] + base) * hit, axis=0, keepdims=True)
        base = base + counted[:, LANES:]
    posi = pos[...].astype(jnp.int32)
    placed = rel * CAP + posi

    loads[0].wait()
    loads[1].wait()
    total = None
    for c in range(3):
        part = vel[c].astype(F32) * mm(coup[...], adj[c])
        total = part if total is None else total + part
    product = jac[...] * jnp.sum(total, axis=0, keepdims=True)

    kmask = (iota((LANES, count), 0) % CAP) == posi
    ids = loc[...]

    def rows_of(value):
        return mm(mt[...], jnp.where(kmask, value, 0.0).astype(BF16), NT)

    id_rows = 64.0 * rows_of((ids // 64).astype(F32)) + rows_of((ids % 64).astype(F32))
    p1, p2, p3 = split3(product)
    p_rows = rows_of(p1.astype(F32)) + (rows_of(p2.astype(F32)) + rows_of(p3.astype(F32)))
    jrow = iota((ndev, LANES), 0) % 8
    jlane = iota((ndev, LANES), 1) // CAP
    is_id = jlane == jrow
    is_p = jlane == (jrow + 4) % 8
    msend[...] = jnp.where(is_id, id_rows, jnp.where(is_p, p_rows, 0.0))

    loads[2].wait()
    loads[3].wait()
    vrow = iota((LANES, LANES), 0)
    for b in range(blocks):
        sl = slice(b * LANES, (b + 1) * LANES)

        def slot8(i, total):
            at = pl.ds(pl.multiple_of(i * 8, 8), 8)
            o8 = off[at, sl]
            m8 = mar[at, sl]
            for k in range(8):
                total = total + jnp.where(o8[k : k + 1] == vrow, m8[k : k + 1], 0.0)
            return total

        built = lax.fori_loop(0, off.shape[0] // 8, slot8, jnp.zeros((LANES, LANES), F32))
        hi, lo = split2(built)
        wt[0:LANES, sl] = hi
        wt[LANES : 2 * LANES, sl] = lo

    pl.semaphore_wait(barrier, ndev - 1)

    def row_copy(src, dst, send_sem, recv_sem, lin):
        return pltpu.make_async_remote_copy(
            src_ref=src, dst_ref=dst, send_sem=send_sem, recv_sem=recv_sem,
            device_id=dev(lin), device_id_type=MESH,
        )

    pltpu.make_async_copy(msend.at[pl.ds(0, 1)], mrecv.at[pl.ds(0, 1)], mrsem).start()

    @pl.loop(1, ndev)
    def _(i):
        j = ndev - i
        row = pl.ds(j, 1)
        row_copy(msend.at[row], mrecv.at[row], msem, mrsem, (me + j) % ndev).start()

    @pl.loop(0, groups)
    def _(i):
        g = groups - 1 - i
        start = pl.multiple_of(g * grows, grows)
        pick = onehot(placed == iota((grows, count), 0) + start).astype(BF16)
        both = mm(pick, wt[...], NT)
        send[pl.ds(start, grows), :] = both[:, :LANES] + both[:, LANES:]

        @pl.loop(0, gsrc)
        def _(q):
            j = g * gsrc + (gsrc - 1 - q)
            at = pl.ds(pl.multiple_of(j * CAP, CAP), CAP)

            @pl.when(j > 0)
            def _():
                row_copy(send.at[at], recv.at[at], ssem, rsem.at[g], (me + j) % ndev).start()

            @pl.when(j == 0)
            def _():
                pltpu.make_async_copy(send.at[at], recv.at[at], rsem.at[g]).start()

    loads[4].wait()

    @pl.loop(0, wx)
    def _(x):
        at = pl.ds(pl.multiple_of(x * wy, wy), wy)
        th[at, :] = jnp.tanh(SHARP * (th[at, :] - THRESHOLD))
        acc[at, :] = jnp.zeros((wy, LANES), F32)

    pltpu.make_async_copy(mrecv, mrecv, mrsem).wait()
    got = mrecv[...]
    chunk_ids = jnp.sum(jnp.where(is_id, got, 0.0).reshape(ndev // 8, 8, LANES), axis=1)
    chunk_p = jnp.sum(jnp.where(is_p, got, 0.0).reshape(ndev // 8, 8, LANES), axis=1)
    plane[...] = pltpu.roll(chunk_p, LANES // 2, axis=1)
    ids_v[...] = chunk_ids.astype(jnp.int32)
    to_smem = pltpu.make_async_copy(ids_v, ids_s, smem_sem)
    to_smem.start()
    to_smem.wait()

    @pl.loop(0, slots // 8)
    def _(r8):
        c = r8 // 16
        l0 = (r8 % 16) * 8
        for k in range(8):
            at = jnp.minimum(jnp.maximum(ids_s[c, l0 + k], 0), voxel_rows - 1)
            rows[pl.ds(pl.multiple_of(r8 * 8, 8) + k, 1), :] = th[pl.ds(at, 1), :]

    eye = iota((LANES, LANES), 0) == iota((LANES, LANES), 1)
    yrow = iota((wy, grows), 0)
    per = 8

    @pl.loop(0, groups)
    def _(i):
        g = groups - 1 - i
        at = pl.ds(pl.multiple_of(g * grows, grows), grows)
        pltpu.make_async_copy(recv.at[at], recv.at[at], rsem.at[g]).wait()
        w = recv[at, :]
        d = jnp.sum((rows[at, :] + T0) * w, axis=1, keepdims=True) * (1.0 / (2.0 * T0))
        halves = grows // LANES
        pcol = []
        idrow = []
        for h in range(halves):
            c = g * halves + h
            dcol = d[h * LANES : (h + 1) * LANES]
            dsend[pl.ds(c, 1), :] = jnp.sum(jnp.where(eye, dcol, 0.0), axis=0, keepdims=True)
            pcol.append(jnp.sum(jnp.where(eye, plane[pl.ds(c, 1), :], 0.0), axis=1, keepdims=True))
            idrow.append(ids_v[pl.ds(c, 1), :])
        p = jnp.concatenate(pcol, axis=0)
        near = RAMP + d
        term = -RAMP * (1.0 + RAMP) / (near * near) * p
        hi, lo = split2(term * w)
        both = jnp.concatenate([hi, lo], axis=1)
        idr = jnp.concatenate(idrow, axis=1)
        xid = idr // wy
        yhot = onehot(yrow == idr % wy)

        @pl.loop(0, gsrc)
        def _(q):
            j = g * gsrc + q
            c = j // 8

            @pl.when(j > 0)
            def _():
                row_copy(
                    dsend.at[pl.ds(c, 1)], drecv.at[pl.ds(j, 1)], dsem, drsem, (me + (ndev - j)) % ndev
                ).start()

            @pl.when(j == 0)
            def _():
                pltpu.make_async_copy(dsend.at[pl.ds(c, 1)], drecv.at[pl.ds(j, 1)], drsem).start()

        @pl.loop(0, wx // per)
        def _(xb):
            pick = jnp.concatenate(
                [jnp.where(xid == xb * per + u, yhot, 0.0) for u in range(per)], axis=0
            ).astype(BF16)
            added = mm(pick, both)
            xs = pl.ds(pl.multiple_of(xb * per * wy, per * wy), per * wy)
            acc[xs, :] = acc[xs, :] + (added[:, :LANES] + added[:, LANES:])

    @pl.loop(0, wx)
    def _(x):
        at = pl.ds(pl.multiple_of(x * wy, wy), wy)
        t = th[at, :]
        ext[x + 2, YO : YO + wy, :] = acc[at, :] * ((SHARP / (2.0 * T0)) * (1.0 - t * t))

    xl, xh = (brick + (nb - 1)) % nb, (brick + 1) % nb
    yl, yh = (dom + (nd - 1)) % nd, (dom + 1) % nd
    ys, y_all = pl.ds(YO, wy), pl.ds(2, wx)
    moves = [
        ((pl.ds(2, 2), ys), (pl.ds(wx + 2, 2), ys), (xl, dom)),
        ((pl.ds(wx, 2), ys), (pl.ds(0, 2), ys), (xh, dom)),
        ((y_all, pl.ds(YO, 2)), (y_all, pl.ds(YO + wy, 2)), (brick, yl)),
        ((y_all, pl.ds(YO + wy - 2, 2)), (y_all, pl.ds(YO - 2, 2)), (brick, yh)),
        ((pl.ds(2, 1), pl.ds(YO, 1)), (pl.ds(wx + 2, 1), pl.ds(YO + wy, 1)), (xl, yl)),
        ((pl.ds(2, 1), pl.ds(YO + wy - 1, 1)), (pl.ds(wx + 2, 1), pl.ds(YO - 1, 1)), (xl, yh)),
        ((pl.ds(wx + 1, 1), pl.ds(YO, 1)), (pl.ds(1, 1), pl.ds(YO + wy, 1)), (xh, yl)),
        ((pl.ds(wx + 1, 1), pl.ds(YO + wy - 1, 1)), (pl.ds(1, 1), pl.ds(YO - 1, 1)), (xh, yh)),
    ]
    halos = [
        pltpu.make_async_remote_copy(
            src_ref=ext.at[s], dst_ref=ext.at[t], send_sem=hsem.at[i], recv_sem=hrsem.at[i],
            device_id=to, device_id_type=MESH,
        )
        for i, (s, t, to) in enumerate(moves)
    ]
    for halo in halos:
        halo.start()
    for halo in halos:
        halo.wait()

    wide = ext.shape[1]
    yline = iota((wide, LANES), 0)
    zline = iota((wide, LANES), 1)
    first_y = jnp.where(dom == 0, YO, 0)
    last_y = jnp.where(dom == nd - 1, YO + wy, wide)
    inside = (yline >= first_y) & (yline < last_y)

    for edge, first_x in ((brick == 0, 0), (brick == nb - 1, wx + 2)):

        @pl.when(edge)
        def _():
            ext[first_x : first_x + 2] = jnp.zeros((2, wide, LANES), F32)

    def around(ref, x):
        y = ref[x]
        total = ref[x + 1] + ref[x - 1]
        total = total + pltpu.roll(y, 1, axis=0) + pltpu.roll(y, wide - 1, axis=0)
        total = total + jnp.where(zline == 0, 0.0, pltpu.roll(y, 1, axis=1))
        total = total + jnp.where(zline == LANES - 1, 0.0, pltpu.roll(y, LANES - 1, axis=1))
        return y, total

    @pl.loop(0, wx + 4)
    def _(x):
        ext[x] = jnp.where(inside, ext[x], 0.0)

    @pl.loop(0, wx + 2)
    def _(x):
        y, near = around(ext, x + 1)
        fst[x + 1] = jnp.where(inside, 0.19 * y + 0.135 * near, 0.0)

    for edge, first_x in ((brick == 0, 1), (brick == nb - 1, wx + 2)):

        @pl.when(edge)
        def _():
            fst[first_x] = jnp.zeros((wide, LANES), F32)

    @pl.loop(0, wx)
    def _(x):
        y, near = around(fst, x + 2)
        new = 0.1 * y + 0.09 * ext[x + 2] + 0.135 * near
        out[x] = new[YO : YO + wy]

    store = pltpu.make_async_copy(out, res_h, osem)
    store.start()

    pltpu.make_async_copy(drecv, drecv, drsem).wait()
    back = jnp.where(is_id, drecv[...], 0.0).T
    spread = None
    for piece in split3(back):
        part = mm(piece, mt[...])
        spread = part if spread is None else spread + part
    den[...] = jnp.sum(jnp.where(kmask, spread, 0.0), axis=0, keepdims=True)

    others = pl.ds(1, ndev - 1)
    row_copy(msend.at[others], mrecv.at[others], msem, mrsem, me).wait_send()
    most = pl.ds(CAP, slots - CAP)
    row_copy(send.at[most], recv.at[most], ssem, rsem.at[0], me).wait_send()
    row_copy(drecv.at[others], drecv.at[others], dsem, drsem, me).wait_send()
    store.wait()


def body(velocity, adjoint, coupling, jac_weight, owner, local_block, offsets, margin, filtered):
    nb, nd = lax.axis_size("brick"), lax.axis_size("dom")
    ndev = nb * nd
    count = owner.shape[0]
    wx, wy, depth = filtered.shape
    slots = ndev * CAP
    wide = wy + 16
    vmem = pl.BlockSpec(memory_space=pltpu.VMEM)
    hbm = pl.BlockSpec(memory_space=pl.ANY)
    dma = pltpu.SemaphoreType.DMA
    result, density = pl.pallas_call(
        functools.partial(kernel, nb, nd, wx, wy),
        out_shape=(
            jax.ShapeDtypeStruct(filtered.shape, F32),
            jax.ShapeDtypeStruct((1, count), F32),
        ),
        in_specs=[vmem] * 4 + [hbm] * 5,
        out_specs=(hbm, vmem),
        scratch_shapes=[
            pltpu.VMEM(velocity.shape, BF16),
            pltpu.VMEM(adjoint.shape, BF16),
            pltpu.VMEM(offsets.shape, jnp.int32),
            pltpu.VMEM(margin.shape, F32),
            pltpu.VMEM((wx * wy, LANES), F32),
            pltpu.VMEM((ndev, count), BF16),
            pltpu.VMEM((1, count), F32),
            pltpu.VMEM((2 * LANES, count), BF16),
            pltpu.VMEM((ndev, LANES), F32),
            pltpu.VMEM((ndev, LANES), F32),
            pltpu.VMEM((slots, LANES), F32),
            pltpu.VMEM((slots, LANES), F32),
            pltpu.VMEM((ndev // 8, LANES), jnp.int32),
            pltpu.SMEM((ndev // 8, LANES), jnp.int32),
            pltpu.VMEM((ndev // 8, LANES), F32),
            pltpu.VMEM((slots, LANES), F32),
            pltpu.VMEM((wx * wy, LANES), F32),
            pltpu.VMEM((ndev // 8, LANES), F32),
            pltpu.VMEM((ndev, LANES), F32),
            pltpu.VMEM((wx + 4, wide, LANES), F32),
            pltpu.VMEM((wx + 4, wide, LANES), F32),
            pltpu.VMEM(filtered.shape, F32),
            dma((5,)), dma, dma, dma, dma, dma((ndev // 16,)), dma, dma, dma((8,)), dma((8,)), dma,
        ],
        compiler_params=pltpu.CompilerParams(
            collective_id=0, has_side_effects=True, vmem_limit_bytes=60 * 1024 * 1024
        ),
        name="sensitivity",
    )(
        coupling, jac_weight.reshape(1, count), owner.reshape(1, count),
        local_block.reshape(1, count), velocity, adjoint, offsets, margin,
        filtered.reshape(wx * wy, depth),
    )
    return result, density.reshape(count)


def solution(mesh):
    return jax.shard_map(
        body,
        mesh=mesh,
        in_specs=(
            P(None, None, ("brick", "dom")),
            P(None, None, ("brick", "dom")),
            P(),
            P(("brick", "dom")),
            P(("brick", "dom"), None),
            P(("brick", "dom")),
            P(None, ("brick", "dom")),
            P(None, ("brick", "dom")),
            P("brick", "dom", None),
        ),
        out_specs=(P("brick", "dom", None), P(("brick", "dom"))),
        check_vma=False,
    )
```

```python
import functools
import math

import jax
import jax.numpy as jnp
from jax import lax
from jax.experimental import pallas as pl
from jax.experimental.pallas import tpu as pltpu
from jax.sharding import PartitionSpec as P

MESH = pl.DeviceIdType.MESH
CAP = 16
LANES = 128
SHARP = 8.0
THRESHOLD = 0.5
T0 = math.tanh(SHARP * THRESHOLD)
RAMP = 0.1
F32 = jnp.float32
BF16 = jnp.bfloat16
YO = 8
NT = (((1,), (1,)), ((), ()))
NN = (((1,), (0,)), ((), ()))


def mm(a, b, dims=NN):
    return lax.dot_general(a, b, dims, preferred_element_type=F32)


def iota(shape, dim):
    return lax.broadcasted_iota(jnp.int32, shape, dim)


def onehot(mask):
    return jnp.where(mask, 1.0, 0.0).astype(F32)


def split2(x):
    hi = x.astype(BF16)
    return hi, (x - hi.astype(F32)).astype(BF16)


def split3(x):
    hi = x.astype(BF16)
    rest = x - hi.astype(F32)
    mid = rest.astype(BF16)
    return hi, mid, (rest - mid.astype(F32)).astype(BF16)


def kernel(
    nb, nd, wx, wy, coup, jac, own, loc, vel_h, adj_h, off_h, mar_h, fil_h,
    res_h, den,
    vel, adj, off, mar, th, mt, pos, wt, fine, parts, msend, mrecv, send, recv, ids_v, ids_s, pcol,
    rows, acc, dsend, drecv, ext, fst, out,
    in_sem, smem_sem, msem, mrsem, ssem, rsem, dsem, drsem, hsem, hrsem, osem,
):
    ndev = nb * nd
    count = own.shape[1]
    blocks = count // LANES
    voxel_rows = wx * wy
    slots = ndev * CAP
    gsrc = 16
    grows = gsrc * CAP
    groups = ndev // gsrc
    brick = lax.axis_index("brick")
    dom = lax.axis_index("dom")
    me = brick * nd + dom

    def dev(lin):
        return (lin // nd, lin % nd)

    loads = [
        pltpu.make_async_copy(h, v, in_sem.at[i])
        for i, (h, v) in enumerate(((vel_h, vel), (adj_h, adj), (off_h, off), (mar_h, mar), (fil_h, th)))
    ]
    for load in loads:
        load.start()

    barrier = pltpu.get_barrier_semaphore()

    @pl.loop(1, ndev)
    def _(i):
        pl.semaphore_signal(
            barrier, inc=1, device_id=dev((me + (ndev - i)) % ndev), device_id_type=MESH
        )

    rel = (own[...] - me + ndev) % ndev
    rr = iota((LANES, 2 * LANES), 0)
    cc = iota((LANES, 2 * LANES), 1)
    upper = onehot((rr < cc) | (cc >= LANES)).astype(BF16)
    hits = [onehot(rel[:, b * LANES : (b + 1) * LANES] == iota((ndev, LANES), 0)) for b in range(blocks)]
    counted = mm(jnp.concatenate(hits, axis=0).astype(BF16), upper)
    base = jnp.zeros((ndev, LANES), F32)
    for b in range(blocks):
        sl = slice(b * LANES, (b + 1) * LANES)
        here = counted[b * ndev : (b + 1) * ndev]
        mt[:, sl] = hits[b].astype(BF16)
        pos[:, sl] = jnp.sum((here[:, :LANES] + base) * hits[b], axis=0, keepdims=True)
        base = base + here[:, LANES:]
    posi = pos[...].astype(jnp.int32)
    placed = rel * CAP + posi

    loads[0].wait()
    loads[1].wait()
    total = None
    for c in range(3):
        part = vel[c].astype(F32) * mm(coup[...], adj[c])
        total = part if total is None else total + part
    product = jac[...] * jnp.sum(total, axis=0, keepdims=True)

    kmask = iota((CAP, count), 0) == posi
    ids = loc[...]
    values = [(ids // 64).astype(F32), (ids % 64).astype(F32)]
    values += [piece.astype(F32) for piece in split3(product)]
    stack = jnp.concatenate([jnp.where(kmask, v, 0.0) for v in values], axis=0).astype(BF16)
    lined = mm(stack, mt[...], NT)
    pieces = [lined[u * CAP : (u + 1) * CAP] for u in range(5)]
    id_rows = jnp.concatenate([64.0 * pieces[0] + pieces[1]] * 8, axis=0).T
    p_rows = jnp.concatenate([pieces[2] + (pieces[3] + pieces[4])] * 8, axis=0).T
    jrow = iota((ndev, LANES), 0) % 8
    jlane = iota((ndev, LANES), 1) // CAP
    is_id = jlane == jrow
    is_p = jlane == (jrow + 4) % 8
    msend[...] = jnp.where(is_id, id_rows, jnp.where(is_p, p_rows, 0.0))

    loads[2].wait()
    loads[3].wait()
    entries = off.shape[0]
    tiles = LANES // 8
    sub = iota((8, LANES), 0)
    for b in range(blocks):
        sl = slice(b * LANES, (b + 1) * LANES)

        @pl.loop(0, entries // 8)
        def _(i):
            at = pl.ds(pl.multiple_of(i * 8, 8), 8)
            o8 = off[at, sl]
            m8 = mar[at, sl]
            fine[at, :] = o8 % 8
            tile = o8 // 8
            for u in range(tiles):
                parts[u, at, :] = jnp.where(tile == u, m8, 0.0)

        def slot8(i, totals):
            totals = list(totals)
            for k in range(8):
                row = pl.ds(i * 8 + k, 1)
                hit = jnp.broadcast_to(fine[row, :], (8, LANES)) == sub
                for u in range(tiles):
                    part = jnp.broadcast_to(parts[u, row, :], (8, LANES))
                    totals[u] = totals[u] + jnp.where(hit, part, 0.0)
            return tuple(totals)

        zero = jnp.zeros((8, LANES), F32)
        built = jnp.concatenate(lax.fori_loop(0, entries // 8, slot8, (zero,) * tiles), axis=0)
        hi, lo = split2(built)
        wt[0:LANES, sl] = hi
        wt[LANES : 2 * LANES, sl] = lo

    prows = min(slots, 512)

    @pl.loop(0, slots // prows)
    def _(g):
        start = pl.multiple_of(g * prows, prows)
        pick = onehot(placed == iota((prows, count), 0) + start).astype(BF16)
        both = mm(pick, wt[...], NT)
        send[pl.ds(start, prows), :] = both[:, :LANES] + both[:, LANES:]

    loads[4].wait()

    @pl.loop(0, wx)
    def _(x):
        at = pl.ds(pl.multiple_of(x * wy, wy), wy)
        th[at, :] = jnp.tanh(SHARP * (th[at, :] - THRESHOLD))
        acc[at, :] = jnp.zeros((wy, LANES), F32)

    pl.semaphore_wait(barrier, ndev - 1)

    def row_copy(src, dst, send_sem, recv_sem, lin):
        return pltpu.make_async_remote_copy(
            src_ref=src, dst_ref=dst, send_sem=send_sem, recv_sem=recv_sem,
            device_id=dev(lin), device_id_type=MESH,
        )

    pltpu.make_async_copy(msend.at[pl.ds(0, 1)], mrecv.at[pl.ds(0, 1)], mrsem).start()

    @pl.loop(1, ndev)
    def _(i):
        j = ndev - i
        row = pl.ds(j, 1)
        row_copy(msend.at[row], mrecv.at[row], msem, mrsem, (me + j) % ndev).start()

    own_rows = pl.ds(0, CAP)
    pltpu.make_async_copy(send.at[own_rows], recv.at[own_rows], rsem.at[0]).start()

    @pl.loop(1, ndev)
    def _(i):
        j = ndev - i
        at = pl.ds(pl.multiple_of(j * CAP, CAP), CAP)
        row_copy(send.at[at], recv.at[at], ssem, rsem.at[j // gsrc], (me + j) % ndev).start()

    pltpu.make_async_copy(mrecv, mrecv, mrsem).wait()
    got = mrecv[...]
    chunk_ids = jnp.sum(jnp.where(is_id, got, 0.0).reshape(ndev // 8, 8, LANES), axis=1)
    chunk_p = jnp.sum(jnp.where(is_p, got, 0.0).reshape(ndev // 8, 8, LANES), axis=1)
    p_lines = pltpu.roll(chunk_p, LANES // 2, axis=1)
    ids_v[...] = chunk_ids.astype(jnp.int32)
    to_smem = pltpu.make_async_copy(ids_v, ids_s, smem_sem)
    to_smem.start()
    to_smem.wait()

    eye = iota((LANES, LANES), 0) == iota((LANES, LANES), 1)
    for c in range(ndev // 8):
        line = jnp.sum(jnp.where(eye, p_lines[c : c + 1], 0.0), axis=1, keepdims=True)
        pcol[c * LANES : (c + 1) * LANES, :] = jnp.broadcast_to(line, (LANES, LANES))

    @pl.loop(0, slots // 8)
    def _(r8):
        c = r8 // 16
        l0 = (r8 % 16) * 8
        for k in range(8):
            at = jnp.minimum(jnp.maximum(ids_s[c, l0 + k], 0), voxel_rows - 1)
            rows[pl.ds(pl.multiple_of(r8 * 8, 8) + k, 1), :] = th[pl.ds(at, 1), :]

    yrow = iota((wy, grows), 0)

    @pl.loop(0, groups)
    def _(i):
        g = groups - 1 - i
        at = pl.ds(pl.multiple_of(g * grows, grows), grows)
        pltpu.make_async_copy(recv.at[at], recv.at[at], rsem.at[g]).wait()
        w = recv[at, :]
        d = jnp.sum((rows[at, :] + T0) * w, axis=1, keepdims=True) * (1.0 / (2.0 * T0))
        halves = grows // LANES
        idrow = []
        for h in range(halves):
            c = g * halves + h
            dcol = d[h * LANES : (h + 1) * LANES]
            dsend[pl.ds(c, 1), :] = jnp.sum(jnp.where(eye, dcol, 0.0), axis=0, keepdims=True)
            idrow.append(ids_v[pl.ds(c, 1), :])
        near = RAMP + d
        term = -RAMP * (1.0 + RAMP) / (near * near) * pcol[at, :]
        hi, lo = split2(term * w)
        both = jnp.concatenate([hi, lo], axis=1)
        idr = jnp.concatenate(idrow, axis=1)
        xid = idr // wy
        yhot = onehot(yrow == idr % wy)

        @pl.loop(0, gsrc)
        def _(q):
            j = g * gsrc + q
            c = j // 8

            @pl.when(j > 0)
            def _():
                row_copy(
                    dsend.at[pl.ds(c, 1)], drecv.at[pl.ds(j, 1)], dsem, drsem, (me + (ndev - j)) % ndev
                ).start()

            @pl.when(j == 0)
            def _():
                pltpu.make_async_copy(dsend.at[pl.ds(c, 1)], drecv.at[pl.ds(j, 1)], drsem).start()

        pick = jnp.concatenate([jnp.where(xid == x, yhot, 0.0) for x in range(wx)], axis=0)
        added = mm(pick.astype(BF16), both)
        acc[...] = acc[...] + (added[:, :LANES] + added[:, LANES:])

    @pl.loop(0, wx)
    def _(x):
        at = pl.ds(pl.multiple_of(x * wy, wy), wy)
        t = th[at, :]
        ext[x + 2, YO : YO + wy, :] = acc[at, :] * ((SHARP / (2.0 * T0)) * (1.0 - t * t))

    xl, xh = (brick + (nb - 1)) % nb, (brick + 1) % nb
    yl, yh = (dom + (nd - 1)) % nd, (dom + 1) % nd
    ys, y_all = pl.ds(YO, wy), pl.ds(2, wx)
    moves = [
        ((pl.ds(2, 2), ys), (pl.ds(wx + 2, 2), ys), (xl, dom)),
        ((pl.ds(wx, 2), ys), (pl.ds(0, 2), ys), (xh, dom)),
        ((y_all, pl.ds(YO, 2)), (y_all, pl.ds(YO + wy, 2)), (brick, yl)),
        ((y_all, pl.ds(YO + wy - 2, 2)), (y_all, pl.ds(YO - 2, 2)), (brick, yh)),
        ((pl.ds(2, 1), pl.ds(YO, 1)), (pl.ds(wx + 2, 1), pl.ds(YO + wy, 1)), (xl, yl)),
        ((pl.ds(2, 1), pl.ds(YO + wy - 1, 1)), (pl.ds(wx + 2, 1), pl.ds(YO - 1, 1)), (xl, yh)),
        ((pl.ds(wx + 1, 1), pl.ds(YO, 1)), (pl.ds(1, 1), pl.ds(YO + wy, 1)), (xh, yl)),
        ((pl.ds(wx + 1, 1), pl.ds(YO + wy - 1, 1)), (pl.ds(1, 1), pl.ds(YO - 1, 1)), (xh, yh)),
    ]
    halos = [
        pltpu.make_async_remote_copy(
            src_ref=ext.at[s], dst_ref=ext.at[t], send_sem=hsem.at[i], recv_sem=hrsem.at[i],
            device_id=to, device_id_type=MESH,
        )
        for i, (s, t, to) in enumerate(moves)
    ]
    for halo in halos:
        halo.start()
    for halo in halos:
        halo.wait()

    for edge, first_x in ((brick == 0, 0), (brick == nb - 1, wx + 2)):

        @pl.when(edge)
        def _():
            ext[first_x : first_x + 2] = jnp.zeros((2, ext.shape[1], LANES), F32)

    for edge, first_y in ((dom == 0, YO - 2), (dom == nd - 1, YO + wy)):

        @pl.when(edge)
        def _():
            @pl.loop(0, wx + 4)
            def _(x):
                ext[x, first_y : first_y + 2, :] = jnp.zeros((2, LANES), F32)

    tall = fst.shape[1]

    def around(ref, x, y0, size):
        y = ref[x, y0 : y0 + size, :]
        zline = iota((size, LANES), 1)
        total = ref[x + 1, y0 : y0 + size, :] + ref[x - 1, y0 : y0 + size, :]
        total = total + ref[x, y0 + 1 : y0 + 1 + size, :] + ref[x, y0 - 1 : y0 - 1 + size, :]
        total = total + jnp.where(zline == 0, 0.0, pltpu.roll(y, 1, axis=1))
        total = total + jnp.where(zline == LANES - 1, 0.0, pltpu.roll(y, LANES - 1, axis=1))
        return y, total

    line = iota((tall, LANES), 0)
    inside = (line >= jnp.where(dom == 0, 1, 0)) & (line <= jnp.where(dom == nd - 1, wy, wy + 1))

    @pl.loop(0, (wx + 2) // 2)
    def _(half):
        for u in range(2):
            x = half * 2 + u + 1
            y, near = around(ext, x, YO - 1, tall)
            fst[x] = jnp.where(inside, 0.19 * y + 0.135 * near, 0.0)

    for edge, first_x in ((brick == 0, 1), (brick == nb - 1, wx + 2)):

        @pl.when(edge)
        def _():
            fst[first_x] = jnp.zeros((tall, LANES), F32)

    @pl.loop(0, wx // 2)
    def _(half):
        for u in range(2):
            x = half * 2 + u
            y, near = around(fst, x + 2, 1, wy)
            out[x] = 0.1 * y + 0.09 * ext[x + 2, YO : YO + wy, :] + 0.135 * near

    store = pltpu.make_async_copy(out, res_h, osem)
    store.start()

    pltpu.make_async_copy(drecv, drecv, drsem).wait()
    back = jnp.where(is_id, drecv[...], 0.0).T
    packed = jnp.sum(back.reshape(LANES // CAP, CAP, ndev), axis=0)
    spread = mm(jnp.concatenate([piece for piece in split3(packed)], axis=0), mt[...])
    spread = spread[:CAP] + (spread[CAP : 2 * CAP] + spread[2 * CAP :])
    den[...] = jnp.sum(jnp.where(kmask, spread, 0.0), axis=0, keepdims=True)

    others = pl.ds(1, ndev - 1)
    row_copy(msend.at[others], mrecv.at[others], msem, mrsem, me).wait_send()
    most = pl.ds(CAP, slots - CAP)
    row_copy(send.at[most], recv.at[most], ssem, rsem.at[0], me).wait_send()
    row_copy(drecv.at[others], drecv.at[others], dsem, drsem, me).wait_send()
    store.wait()


def body(velocity, adjoint, coupling, jac_weight, owner, local_block, offsets, margin, filtered):
    nb, nd = lax.axis_size("brick"), lax.axis_size("dom")
    ndev = nb * nd
    count = owner.shape[0]
    wx, wy, depth = filtered.shape
    slots = ndev * CAP
    wide = wy + 16
    vmem = pl.BlockSpec(memory_space=pltpu.VMEM)
    hbm = pl.BlockSpec(memory_space=pl.ANY)
    dma = pltpu.SemaphoreType.DMA
    result, density = pl.pallas_call(
        functools.partial(kernel, nb, nd, wx, wy),
        out_shape=(
            jax.ShapeDtypeStruct(filtered.shape, F32),
            jax.ShapeDtypeStruct((1, count), F32),
        ),
        in_specs=[vmem] * 4 + [hbm] * 5,
        out_specs=(hbm, vmem),
        scratch_shapes=[
            pltpu.VMEM(velocity.shape, BF16),
            pltpu.VMEM(adjoint.shape, BF16),
            pltpu.VMEM(offsets.shape, jnp.int32),
            pltpu.VMEM(margin.shape, F32),
            pltpu.VMEM((wx * wy, LANES), F32),
            pltpu.VMEM((ndev, count), BF16),
            pltpu.VMEM((1, count), F32),
            pltpu.VMEM((2 * LANES, count), BF16),
            pltpu.VMEM((offsets.shape[0], LANES), jnp.int32),
            pltpu.VMEM((LANES // 8, offsets.shape[0], LANES), F32),
            pltpu.VMEM((ndev, LANES), F32),
            pltpu.VMEM((ndev, LANES), F32),
            pltpu.VMEM((slots, LANES), F32),
            pltpu.VMEM((slots, LANES), F32),
            pltpu.VMEM((ndev // 8, LANES), jnp.int32),
            pltpu.SMEM((ndev // 8, LANES), jnp.int32),
            pltpu.VMEM((slots, LANES), F32),
            pltpu.VMEM((slots, LANES), F32),
            pltpu.VMEM((wx * wy, LANES), F32),
            pltpu.VMEM((ndev // 8, LANES), F32),
            pltpu.VMEM((ndev, LANES), F32),
            pltpu.VMEM((wx + 4, wide, LANES), F32),
            pltpu.VMEM((wx + 4, wy + 8, LANES), F32),
            pltpu.VMEM(filtered.shape, F32),
            dma((5,)), dma, dma, dma, dma, dma((ndev // 16,)), dma, dma, dma((8,)), dma((8,)), dma,
        ],
        compiler_params=pltpu.CompilerParams(
            collective_id=0, has_side_effects=True, vmem_limit_bytes=60 * 1024 * 1024
        ),
        name="sensitivity",
    )(
        coupling, jac_weight.reshape(1, count), owner.reshape(1, count),
        local_block.reshape(1, count), velocity, adjoint, offsets, margin,
        filtered.reshape(wx * wy, depth),
    )
    return result, density.reshape(count)


def solution(mesh):
    return jax.shard_map(
        body,
        mesh=mesh,
        in_specs=(
            P(None, None, ("brick", "dom")),
            P(None, None, ("brick", "dom")),
            P(),
            P(("brick", "dom")),
            P(("brick", "dom"), None),
            P(("brick", "dom")),
            P(None, ("brick", "dom")),
            P(None, ("brick", "dom")),
            P("brick", "dom", None),
        ),
        out_specs=(P("brick", "dom", None), P(("brick", "dom"))),
        check_vma=False,
    )
```

```python
import functools
import math

import jax
import jax.numpy as jnp
from jax import lax
from jax.experimental import pallas as pl
from jax.experimental.pallas import tpu as pltpu
from jax.sharding import PartitionSpec as P

MESH = pl.DeviceIdType.MESH
CAP = 16
LANES = 128
SHARP = 8.0
THRESHOLD = 0.5
T0 = math.tanh(SHARP * THRESHOLD)
RAMP = 0.1
F32 = jnp.float32
BF16 = jnp.bfloat16
YO = 8
NT = (((1,), (1,)), ((), ()))
NN = (((1,), (0,)), ((), ()))


def mm(a, b, dims=NN):
    return lax.dot_general(a, b, dims, preferred_element_type=F32)


def iota(shape, dim):
    return lax.broadcasted_iota(jnp.int32, shape, dim)


def onehot(mask):
    return jnp.where(mask, 1.0, 0.0).astype(F32)


def split2(x):
    hi = x.astype(BF16)
    return hi, (x - hi.astype(F32)).astype(BF16)


def split3(x):
    hi = x.astype(BF16)
    rest = x - hi.astype(F32)
    mid = rest.astype(BF16)
    return hi, mid, (rest - mid.astype(F32)).astype(BF16)


def kernel(
    nb, nd, wx, wy, coup, jac, own, loc, vel_h, adj_h, off_h, mar_h, fil_h,
    res_h, den,
    vel, adj, off, mar, th, mt, pos, wt, fine, parts, msend, mrecv, send, recv, ids_v, ids_s, pcol,
    rows, acc, dsend, drecv, ext, fst, out,
    in_sem, smem_sem, msem, mrsem, ssem, rsem, dsem, drsem, hsem, hrsem, osem,
):
    ndev = nb * nd
    count = own.shape[1]
    blocks = count // LANES
    voxel_rows = wx * wy
    slots = ndev * CAP
    gsrc = 16
    grows = gsrc * CAP
    groups = ndev // gsrc
    brick = lax.axis_index("brick")
    dom = lax.axis_index("dom")

    def ahead(db, dd):
        return (brick + db) & (nb - 1), (dom + dd) & (nd - 1)

    def behind(db, dd):
        return (brick - db) & (nb - 1), (dom - dd) & (nd - 1)

    def others_in_turn(act):
        @pl.loop(1, nb)
        def _(i):
            for dd in reversed(range(nd)):
                act(nb - i, dd)

        for dd in reversed(range(1, nd)):
            act(0, dd)

    loads = [
        pltpu.make_async_copy(h, v, in_sem.at[i])
        for i, (h, v) in enumerate(((vel_h, vel), (adj_h, adj), (off_h, off), (mar_h, mar), (fil_h, th)))
    ]
    for load in loads:
        load.start()

    barrier = pltpu.get_barrier_semaphore()

    def greet(db, dd):
        pl.semaphore_signal(barrier, inc=1, device_id=ahead(db, dd), device_id_type=MESH)

    others_in_turn(greet)

    owners = own[...]
    rel = ((owners // nd - brick) & (nb - 1)) * nd + ((owners % nd - dom) & (nd - 1))
    rr = iota((LANES, 2 * LANES), 0)
    cc = iota((LANES, 2 * LANES), 1)
    upper = onehot((rr < cc) | (cc >= LANES)).astype(BF16)
    hits = [onehot(rel[:, b * LANES : (b + 1) * LANES] == iota((ndev, LANES), 0)) for b in range(blocks)]
    counted = mm(jnp.concatenate(hits, axis=0).astype(BF16), upper)
    base = jnp.zeros((ndev, LANES), F32)
    for b in range(blocks):
        sl = slice(b * LANES, (b + 1) * LANES)
        here = counted[b * ndev : (b + 1) * ndev]
        mt[:, sl] = hits[b].astype(BF16)
        pos[:, sl] = jnp.sum((here[:, :LANES] + base) * hits[b], axis=0, keepdims=True)
        base = base + here[:, LANES:]
    posi = pos[...].astype(jnp.int32)
    placed = rel * CAP + posi

    loads[0].wait()
    loads[1].wait()
    total = None
    for c in range(3):
        part = vel[c].astype(F32) * mm(coup[...], adj[c])
        total = part if total is None else total + part
    product = jac[...] * jnp.sum(total, axis=0, keepdims=True)

    kmask = iota((CAP, count), 0) == posi
    ids = loc[...]
    values = [(ids // 64).astype(F32), (ids % 64).astype(F32)]
    values += [piece.astype(F32) for piece in split3(product)]
    stack = jnp.concatenate([jnp.where(kmask, v, 0.0) for v in values], axis=0).astype(BF16)
    lined = mm(stack, mt[...], NT)
    pieces = [lined[u * CAP : (u + 1) * CAP] for u in range(5)]
    id_rows = jnp.concatenate([64.0 * pieces[0] + pieces[1]] * 8, axis=0).T
    p_rows = jnp.concatenate([pieces[2] + (pieces[3] + pieces[4])] * 8, axis=0).T
    jrow = iota((ndev, LANES), 0) % 8
    jlane = iota((ndev, LANES), 1) // CAP
    is_id = jlane == jrow
    is_p = jlane == (jrow + 4) % 8
    msend[...] = jnp.where(is_id, id_rows, jnp.where(is_p, p_rows, 0.0))

    loads[2].wait()
    loads[3].wait()
    entries = off.shape[0]
    tiles = LANES // 8
    sub = iota((8, LANES), 0)
    for b in range(blocks):
        sl = slice(b * LANES, (b + 1) * LANES)

        @pl.loop(0, entries // 8)
        def _(i):
            at = pl.ds(pl.multiple_of(i * 8, 8), 8)
            o8 = off[at, sl]
            m8 = mar[at, sl]
            fine[at, :] = o8 % 8
            tile = o8 // 8
            for u in range(tiles):
                parts[u, at, :] = jnp.where(tile == u, m8, 0.0)

        def slot8(i, totals):
            totals = list(totals)
            for k in range(8):
                row = pl.ds(i * 8 + k, 1)
                hit = jnp.broadcast_to(fine[row, :], (8, LANES)) == sub
                for u in range(tiles):
                    part = jnp.broadcast_to(parts[u, row, :], (8, LANES))
                    totals[u] = totals[u] + jnp.where(hit, part, 0.0)
            return tuple(totals)

        zero = jnp.zeros((8, LANES), F32)
        built = jnp.concatenate(lax.fori_loop(0, entries // 8, slot8, (zero,) * tiles), axis=0)
        hi, lo = split2(built.T)
        wt[sl, 0:LANES] = hi
        wt[sl, LANES : 2 * LANES] = lo

    pick = onehot(placed == iota((slots, count), 0)).astype(BF16)
    both = mm(pick, wt[...])
    send[...] = both[:, :LANES] + both[:, LANES:]

    loads[4].wait()

    pl.semaphore_wait(barrier, ndev - 1)

    def row_copy(src, dst, send_sem, recv_sem, to):
        return pltpu.make_async_remote_copy(
            src_ref=src, dst_ref=dst, send_sem=send_sem, recv_sem=recv_sem,
            device_id=to, device_id_type=MESH,
        )

    pltpu.make_async_copy(msend.at[pl.ds(0, 1)], mrecv.at[pl.ds(0, 1)], mrsem).start()

    def send_meta(db, dd):
        row = pl.ds(db * nd + dd, 1)
        row_copy(msend.at[row], mrecv.at[row], msem, mrsem, ahead(db, dd)).start()

    others_in_turn(send_meta)

    own_rows = pl.ds(0, CAP)
    pltpu.make_async_copy(send.at[own_rows], recv.at[own_rows], rsem.at[0]).start()

    def send_maps(db, dd):
        at = pl.ds(pl.multiple_of((db * nd + dd) * CAP, CAP), CAP)
        row_copy(
            send.at[at], recv.at[at], ssem, rsem.at[db * nd // gsrc], ahead(db, dd)
        ).start()

    others_in_turn(send_maps)

    @pl.loop(0, wx)
    def _(x):
        at = pl.ds(pl.multiple_of(x * wy, wy), wy)
        th[at, :] = jnp.tanh(SHARP * (th[at, :] - THRESHOLD))
        acc[at, :] = jnp.zeros((wy, LANES), F32)

    pltpu.make_async_copy(mrecv, mrecv, mrsem).wait()
    got = mrecv[...]
    chunk_ids = jnp.sum(jnp.where(is_id, got, 0.0).reshape(ndev // 8, 8, LANES), axis=1)
    chunk_p = jnp.sum(jnp.where(is_p, got, 0.0).reshape(ndev // 8, 8, LANES), axis=1)
    p_lines = pltpu.roll(chunk_p, LANES // 2, axis=1)
    ids_v[...] = chunk_ids.astype(jnp.int32)
    to_smem = pltpu.make_async_copy(ids_v, ids_s, smem_sem)
    to_smem.start()
    to_smem.wait()

    eye = iota((LANES, LANES), 0) == iota((LANES, LANES), 1)
    for c in range(ndev // 8):
        line = jnp.sum(jnp.where(eye, p_lines[c : c + 1], 0.0), axis=1, keepdims=True)
        pcol[c * LANES : (c + 1) * LANES, :] = jnp.broadcast_to(line, (LANES, LANES))

    @pl.loop(0, slots // LANES)
    def _(c):
        for k in range(LANES):
            at = ids_s[c, k] & (voxel_rows - 1)
            rows[pl.ds(c * LANES + k, 1), :] = th[pl.ds(at, 1), :]

    yrow = iota((wy, grows), 0)

    @pl.loop(0, groups)
    def _(i):
        g = groups - 1 - i
        at = pl.ds(pl.multiple_of(g * grows, grows), grows)
        pltpu.make_async_copy(recv.at[at], recv.at[at], rsem.at[g]).wait()
        w = recv[at, :]
        d = jnp.sum((rows[at, :] + T0) * w, axis=1, keepdims=True) * (1.0 / (2.0 * T0))
        halves = grows // LANES
        idrow = []
        for h in range(halves):
            c = g * halves + h
            dcol = d[h * LANES : (h + 1) * LANES]
            dsend[pl.ds(c, 1), :] = jnp.sum(jnp.where(eye, dcol, 0.0), axis=0, keepdims=True)
            idrow.append(ids_v[pl.ds(c, 1), :])
        near = RAMP + d
        term = -RAMP * (1.0 + RAMP) / (near * near) * pcol[at, :]
        hi, lo = split2(term * w)
        both = jnp.concatenate([hi, lo], axis=1)
        idr = jnp.concatenate(idrow, axis=1)
        xid = idr // wy
        yhot = onehot(yrow == idr % wy)

        for q in range(gsrc):
            db = g * (gsrc // nd) + q // nd
            dd = q % nd
            c = g * (gsrc // 8) + q // 8
            back = row_copy(
                dsend.at[pl.ds(c, 1)], drecv.at[pl.ds(g * gsrc + q, 1)], dsem, drsem, behind(db, dd)
            )
            if q:
                back.start()
            else:
                pl.when(g > 0)(back.start)

        pick = jnp.concatenate([jnp.where(xid == x, yhot, 0.0) for x in range(wx)], axis=0)
        added = mm(pick.astype(BF16), both)
        acc[...] = acc[...] + (added[:, :LANES] + added[:, LANES:])

    @pl.loop(0, wx)
    def _(x):
        at = pl.ds(pl.multiple_of(x * wy, wy), wy)
        t = th[at, :]
        ext[x + 2, YO : YO + wy, :] = acc[at, :] * ((SHARP / (2.0 * T0)) * (1.0 - t * t))

    xl, xh = (brick + (nb - 1)) % nb, (brick + 1) % nb
    yl, yh = (dom + (nd - 1)) % nd, (dom + 1) % nd
    ys, y_all = pl.ds(YO, wy), pl.ds(2, wx)
    moves = [
        ((pl.ds(2, 2), ys), (pl.ds(wx + 2, 2), ys), (xl, dom)),
        ((pl.ds(wx, 2), ys), (pl.ds(0, 2), ys), (xh, dom)),
        ((y_all, pl.ds(YO, 2)), (y_all, pl.ds(YO + wy, 2)), (brick, yl)),
        ((y_all, pl.ds(YO + wy - 2, 2)), (y_all, pl.ds(YO - 2, 2)), (brick, yh)),
        ((pl.ds(2, 1), pl.ds(YO, 1)), (pl.ds(wx + 2, 1), pl.ds(YO + wy, 1)), (xl, yl)),
        ((pl.ds(2, 1), pl.ds(YO + wy - 1, 1)), (pl.ds(wx + 2, 1), pl.ds(YO - 1, 1)), (xl, yh)),
        ((pl.ds(wx + 1, 1), pl.ds(YO, 1)), (pl.ds(1, 1), pl.ds(YO + wy, 1)), (xh, yl)),
        ((pl.ds(wx + 1, 1), pl.ds(YO + wy - 1, 1)), (pl.ds(1, 1), pl.ds(YO - 1, 1)), (xh, yh)),
    ]
    halos = [
        pltpu.make_async_remote_copy(
            src_ref=ext.at[s], dst_ref=ext.at[t], send_sem=hsem.at[i], recv_sem=hrsem.at[i],
            device_id=to, device_id_type=MESH,
        )
        for i, (s, t, to) in enumerate(moves)
    ]
    for halo in halos:
        halo.start()

    tall = fst.shape[1]

    def around(ref, x, y0, size):
        y = ref[x, y0 : y0 + size, :]
        zline = iota((size, LANES), 1)
        total = ref[x + 1, y0 : y0 + size, :] + ref[x - 1, y0 : y0 + size, :]
        total = total + ref[x, y0 + 1 : y0 + 1 + size, :] + ref[x, y0 - 1 : y0 - 1 + size, :]
        total = total + jnp.where(zline == 0, 0.0, pltpu.roll(y, 1, axis=1))
        total = total + jnp.where(zline == LANES - 1, 0.0, pltpu.roll(y, LANES - 1, axis=1))
        return y, total

    def first_sweep(x, row, size):
        y, near = around(ext, x, YO - 1 + row, size)
        fst[x, row : row + size, :] = 0.19 * y + 0.135 * near

    def in_steps(start, stop, step, act):
        @pl.loop(0, (stop - start) // step)
        def _(i):
            for u in range(step):
                act(start + i * step + u)

        for x in range(start + (stop - start) // step * step, stop):
            act(x)

    in_steps(3, wx + 1, 4, lambda x: first_sweep(x, 8, wy - 8))
    for halo in halos:
        halo.wait()

    for edge, first_x in ((brick == 0, 0), (brick == nb - 1, wx + 2)):

        @pl.when(edge)
        def _():
            ext[first_x : first_x + 2] = jnp.zeros((2, ext.shape[1], LANES), F32)

    for edge, first_y in ((dom == 0, YO - 2), (dom == nd - 1, YO + wy)):

        @pl.when(edge)
        def _():
            @pl.loop(0, wx + 4)
            def _(x):
                ext[x, first_y : first_y + 2, :] = jnp.zeros((2, LANES), F32)

    def rims(x):
        first_sweep(x, 0, 8)
        first_sweep(x, wy, 8)

    for x in (1, 2, wx + 1, wx + 2):
        first_sweep(x, 0, tall)
    in_steps(3, wx + 1, 4, rims)

    for edge, row in ((dom == 0, 0), (dom == nd - 1, wy + 1)):

        @pl.when(edge)
        def _():
            @pl.loop(1, wx + 3)
            def _(x):
                fst[x, row : row + 1, :] = jnp.zeros((1, LANES), F32)

    for edge, first_x in ((brick == 0, 1), (brick == nb - 1, wx + 2)):

        @pl.when(edge)
        def _():
            fst[first_x] = jnp.zeros((tall, LANES), F32)

    def second_sweep(x):
        y, near = around(fst, x + 2, 1, wy)
        out[x] = 0.1 * y + 0.09 * ext[x + 2, YO : YO + wy, :] + 0.135 * near

    in_steps(0, wx, 4, second_sweep)

    store = pltpu.make_async_copy(out, res_h, osem)
    store.start()

    pltpu.make_async_copy(dsend.at[pl.ds(0, 1)], drecv.at[pl.ds(0, 1)], drsem).start()

    pltpu.make_async_copy(drecv, drecv, drsem).wait()
    back = jnp.where(is_id, drecv[...], 0.0).T
    packed = jnp.sum(back.reshape(LANES // CAP, CAP, ndev), axis=0)
    spread = mm(jnp.concatenate([piece for piece in split3(packed)], axis=0), mt[...])
    spread = spread[:CAP] + (spread[CAP : 2 * CAP] + spread[2 * CAP :])
    den[...] = jnp.sum(jnp.where(kmask, spread, 0.0), axis=0, keepdims=True)

    others = pl.ds(1, ndev - 1)
    row_copy(msend.at[others], mrecv.at[others], msem, mrsem, (brick, dom)).wait_send()
    most = pl.ds(CAP, slots - CAP)
    row_copy(send.at[most], recv.at[most], ssem, rsem.at[0], (brick, dom)).wait_send()
    row_copy(drecv.at[others], drecv.at[others], dsem, drsem, (brick, dom)).wait_send()
    store.wait()


def body(velocity, adjoint, coupling, jac_weight, owner, local_block, offsets, margin, filtered):
    nb, nd = lax.axis_size("brick"), lax.axis_size("dom")
    ndev = nb * nd
    count = owner.shape[0]
    wx, wy, depth = filtered.shape
    slots = ndev * CAP
    wide = wy + 16
    vmem = pl.BlockSpec(memory_space=pltpu.VMEM)
    hbm = pl.BlockSpec(memory_space=pl.ANY)
    dma = pltpu.SemaphoreType.DMA
    result, density = pl.pallas_call(
        functools.partial(kernel, nb, nd, wx, wy),
        out_shape=(
            jax.ShapeDtypeStruct(filtered.shape, F32),
            jax.ShapeDtypeStruct((1, count), F32),
        ),
        in_specs=[vmem] * 4 + [hbm] * 5,
        out_specs=(hbm, vmem),
        scratch_shapes=[
            pltpu.VMEM(velocity.shape, BF16),
            pltpu.VMEM(adjoint.shape, BF16),
            pltpu.VMEM(offsets.shape, jnp.int32),
            pltpu.VMEM(margin.shape, F32),
            pltpu.VMEM((wx * wy, LANES), F32),
            pltpu.VMEM((ndev, count), BF16),
            pltpu.VMEM((1, count), F32),
            pltpu.VMEM((count, 2 * LANES), BF16),
            pltpu.VMEM((offsets.shape[0], LANES), jnp.int32),
            pltpu.VMEM((LANES // 8, offsets.shape[0], LANES), F32),
            pltpu.VMEM((ndev, LANES), F32),
            pltpu.VMEM((ndev, LANES), F32),
            pltpu.VMEM((slots, LANES), F32),
            pltpu.VMEM((slots, LANES), F32),
            pltpu.VMEM((ndev // 8, LANES), jnp.int32),
            pltpu.SMEM((ndev // 8, LANES), jnp.int32),
            pltpu.VMEM((slots, LANES), F32),
            pltpu.VMEM((slots, LANES), F32),
            pltpu.VMEM((wx * wy, LANES), F32),
            pltpu.VMEM((ndev // 8, LANES), F32),
            pltpu.VMEM((ndev, LANES), F32),
            pltpu.VMEM((wx + 4, wide, LANES), F32),
            pltpu.VMEM((wx + 4, wy + 8, LANES), F32),
            pltpu.VMEM(filtered.shape, F32),
            dma((5,)), dma, dma, dma, dma, dma((ndev // 16,)), dma, dma, dma((8,)), dma((8,)), dma,
        ],
        compiler_params=pltpu.CompilerParams(
            collective_id=0, has_side_effects=True, vmem_limit_bytes=60 * 1024 * 1024
        ),
        name="sensitivity",
    )(
        coupling, jac_weight.reshape(1, count), owner.reshape(1, count),
        local_block.reshape(1, count), velocity, adjoint, offsets, margin,
        filtered.reshape(wx * wy, depth),
    )
    return result, density.reshape(count)


def solution(mesh):
    return jax.shard_map(
        body,
        mesh=mesh,
        in_specs=(
            P(None, None, ("brick", "dom")),
            P(None, None, ("brick", "dom")),
            P(),
            P(("brick", "dom")),
            P(("brick", "dom"), None),
            P(("brick", "dom")),
            P(None, ("brick", "dom")),
            P(None, ("brick", "dom")),
            P("brick", "dom", None),
        ),
        out_specs=(P("brick", "dom", None), P(("brick", "dom"))),
        check_vma=False,
    )
```

```python
import functools
import math

import jax
import jax.numpy as jnp
from jax import lax
from jax.experimental import pallas as pl
from jax.experimental.pallas import tpu as pltpu
from jax.sharding import PartitionSpec as P

MESH = pl.DeviceIdType.MESH
CAP = 16
LANES = 128
SHARP = 8.0
THRESHOLD = 0.5
T0 = math.tanh(SHARP * THRESHOLD)
RAMP = 0.1
F32 = jnp.float32
BF16 = jnp.bfloat16
YO = 8
NT = (((1,), (1,)), ((), ()))
NN = (((1,), (0,)), ((), ()))


def mm(a, b, dims=NN):
    return lax.dot_general(a, b, dims, preferred_element_type=F32)


def iota(shape, dim):
    return lax.broadcasted_iota(jnp.int32, shape, dim)


def onehot(mask):
    return jnp.where(mask, 1.0, 0.0).astype(F32)


def split2(x):
    hi = x.astype(BF16)
    return hi, (x - hi.astype(F32)).astype(BF16)


def split3(x):
    hi = x.astype(BF16)
    rest = x - hi.astype(F32)
    mid = rest.astype(BF16)
    return hi, mid, (rest - mid.astype(F32)).astype(BF16)


def kernel(
    nb, nd, wx, wy, coup, jac, own, loc, vel_h, adj_h, off_h, mar_h, fil_h,
    res_h, den,
    vel, adj, off, mar, th, mt, pos, wt, fine, parts, msend, mrecv, send, recv, ids_v, ids_s, pcol,
    rows, acc, dsend, drecv, ext, fst, out,
    in_sem, smem_sem, msem, mrsem, ssem, rsem, dsem, drsem, hsem, hrsem, osem,
):
    ndev = nb * nd
    count = own.shape[1]
    blocks = count // LANES
    voxel_rows = wx * wy
    slots = ndev * CAP
    xn, zn, yn = nb // 2, nd // 4, 4
    gsrc = xn * yn
    grows = gsrc * CAP
    groups = 2 * zn
    brick = lax.axis_index("brick")
    dom = lax.axis_index("dom")
    xi, ci, zi, yi = brick // 2, brick % 2, dom // yn, dom % yn

    def ahead(g, m):
        p, q = m // yn, m % yn
        r = p + q + (g & (zn - 1))
        return (
            ((xi + p) & (xn - 1)) * 2 + ((ci + g // zn) & 1),
            ((zi + r) & (zn - 1)) * yn + ((yi + q) & (yn - 1)),
        )

    def behind(g, m):
        p, q = m // yn, m % yn
        r = p + q + (g & (zn - 1))
        return (
            ((xi - p) & (xn - 1)) * 2 + ((ci - g // zn) & 1),
            ((zi - r) & (zn - 1)) * yn + ((yi - q) & (yn - 1)),
        )

    def others_in_turn(act):
        @pl.loop(1, groups)
        def _(i):
            for m in reversed(range(gsrc)):
                act(groups - i, m)

        for m in reversed(range(1, gsrc)):
            act(0, m)

    loads = [
        pltpu.make_async_copy(h, v, in_sem.at[i])
        for i, (h, v) in enumerate(((vel_h, vel), (adj_h, adj), (off_h, off), (mar_h, mar), (fil_h, th)))
    ]
    for load in loads:
        load.start()

    barrier = pltpu.get_barrier_semaphore()

    def greet(g, m):
        pl.semaphore_signal(barrier, inc=1, device_id=ahead(g, m), device_id_type=MESH)

    others_in_turn(greet)

    owners = own[...]
    obrick, odom = owners // nd, owners % nd
    op = (obrick // 2 - xi) & (xn - 1)
    oq = (odom % yn - yi) & (yn - 1)
    ok = (odom // yn - zi - op - oq) & (zn - 1)
    rel = ((((obrick % 2 - ci) & 1) * zn + ok) * xn + op) * yn + oq
    rr = iota((LANES, 2 * LANES), 0)
    cc = iota((LANES, 2 * LANES), 1)
    upper = onehot((rr < cc) | (cc >= LANES)).astype(BF16)
    hits = [onehot(rel[:, b * LANES : (b + 1) * LANES] == iota((ndev, LANES), 0)) for b in range(blocks)]
    counted = mm(jnp.concatenate(hits, axis=0).astype(BF16), upper)
    base = jnp.zeros((ndev, LANES), F32)
    for b in range(blocks):
        sl = slice(b * LANES, (b + 1) * LANES)
        here = counted[b * ndev : (b + 1) * ndev]
        mt[:, sl] = hits[b].astype(BF16)
        pos[:, sl] = jnp.sum((here[:, :LANES] + base) * hits[b], axis=0, keepdims=True)
        base = base + here[:, LANES:]
    posi = pos[...].astype(jnp.int32)
    placed = rel * CAP + posi

    loads[0].wait()
    loads[1].wait()
    total = None
    for c in range(3):
        part = vel[c].astype(F32) * mm(coup[...], adj[c])
        total = part if total is None else total + part
    product = jac[...] * jnp.sum(total, axis=0, keepdims=True)

    kmask = iota((CAP, count), 0) == posi
    ids = loc[...]
    values = [(ids // 64).astype(F32), (ids % 64).astype(F32)]
    values += [piece.astype(F32) for piece in split3(product)]
    stack = jnp.concatenate([jnp.where(kmask, v, 0.0) for v in values], axis=0).astype(BF16)
    lined = mm(stack, mt[...], NT)
    pieces = [lined[u * CAP : (u + 1) * CAP] for u in range(5)]
    id_rows = jnp.concatenate([64.0 * pieces[0] + pieces[1]] * 8, axis=0).T
    p_rows = jnp.concatenate([pieces[2] + (pieces[3] + pieces[4])] * 8, axis=0).T
    jrow = iota((ndev, LANES), 0) % 8
    jlane = iota((ndev, LANES), 1) // CAP
    is_id = jlane == jrow
    is_p = jlane == (jrow + 4) % 8
    msend[...] = jnp.where(is_id, id_rows, jnp.where(is_p, p_rows, 0.0))

    loads[2].wait()
    loads[3].wait()
    entries = off.shape[0]
    tiles = LANES // 8
    sub = iota((8, LANES), 0)
    for b in range(blocks):
        sl = slice(b * LANES, (b + 1) * LANES)

        @pl.loop(0, entries // 8, unroll=2)
        def _(i):
            at = pl.ds(pl.multiple_of(i * 8, 8), 8)
            o8 = off[at, sl]
            m8 = mar[at, sl]
            fine[at, :] = o8 & 7
            tile = o8 >> 3
            for u in range(tiles):
                parts[u, at, :] = jnp.where(tile == u, m8, 0.0)

        def slot8(i, totals):
            totals = list(totals)
            for k in range(8):
                row = pl.ds(i * 8 + k, 1)
                hit = jnp.broadcast_to(fine[row, :], (8, LANES)) == sub
                for u in range(tiles):
                    part = jnp.broadcast_to(parts[u, row, :], (8, LANES))
                    totals[u] = totals[u] + jnp.where(hit, part, 0.0)
            return tuple(totals)

        zero = jnp.zeros((8, LANES), F32)
        built = jnp.concatenate(lax.fori_loop(0, entries // 8, slot8, (zero,) * tiles, unroll=2), axis=0)
        hi, lo = split2(built.T)
        wt[sl, 0:LANES] = hi
        wt[sl, LANES : 2 * LANES] = lo

    pick = onehot(placed == iota((slots, count), 0)).astype(BF16)
    both = mm(pick, wt[...])
    send[...] = both[:, :LANES] + both[:, LANES:]

    loads[4].wait()

    pl.semaphore_wait(barrier, ndev - 1)

    def row_copy(src, dst, send_sem, recv_sem, to):
        return pltpu.make_async_remote_copy(
            src_ref=src, dst_ref=dst, send_sem=send_sem, recv_sem=recv_sem,
            device_id=to, device_id_type=MESH,
        )

    pltpu.make_async_copy(msend.at[pl.ds(0, 1)], mrecv.at[pl.ds(0, 1)], mrsem).start()

    def send_meta(g, m):
        row = pl.ds(g * gsrc + m, 1)
        row_copy(msend.at[row], mrecv.at[row], msem, mrsem, ahead(g, m)).start()

    others_in_turn(send_meta)

    own_rows = pl.ds(0, CAP)
    pltpu.make_async_copy(send.at[own_rows], recv.at[own_rows], rsem.at[0]).start()

    def send_maps(g, m):
        at = pl.ds(pl.multiple_of((g * gsrc + m) * CAP, CAP), CAP)
        row_copy(send.at[at], recv.at[at], ssem, rsem.at[g], ahead(g, m)).start()

    others_in_turn(send_maps)

    @pl.loop(0, wx)
    def _(x):
        at = pl.ds(pl.multiple_of(x * wy, wy), wy)
        th[at, :] = jnp.tanh(SHARP * (th[at, :] - THRESHOLD))
        acc[at, :] = jnp.zeros((wy, LANES), F32)

    pltpu.make_async_copy(mrecv, mrecv, mrsem).wait()
    got = mrecv[...]
    chunk_ids = jnp.sum(jnp.where(is_id, got, 0.0).reshape(ndev // 8, 8, LANES), axis=1)
    chunk_p = jnp.sum(jnp.where(is_p, got, 0.0).reshape(ndev // 8, 8, LANES), axis=1)
    p_lines = pltpu.roll(chunk_p, LANES // 2, axis=1)
    ids_v[...] = chunk_ids.astype(jnp.int32)
    to_smem = pltpu.make_async_copy(ids_v, ids_s, smem_sem)
    to_smem.start()
    to_smem.wait()

    eye = iota((LANES, LANES), 0) == iota((LANES, LANES), 1)
    for c in range(ndev // 8):
        line = jnp.sum(jnp.where(eye, p_lines[c : c + 1], 0.0), axis=1, keepdims=True)
        pcol[c * LANES : (c + 1) * LANES, :] = jnp.broadcast_to(line, (LANES, LANES))

    @pl.loop(0, slots // LANES)
    def _(c):
        for k in range(LANES):
            at = ids_s[c, k] & (voxel_rows - 1)
            rows[pl.ds(c * LANES + k, 1), :] = th[pl.ds(at, 1), :]

    yrow = iota((wy, grows), 0)

    @pl.loop(0, groups)
    def _(i):
        g = groups - 1 - i
        at = pl.ds(pl.multiple_of(g * grows, grows), grows)
        pltpu.make_async_copy(recv.at[at], recv.at[at], rsem.at[g]).wait()
        w = recv[at, :]
        d = jnp.sum((rows[at, :] + T0) * w, axis=1, keepdims=True) * (1.0 / (2.0 * T0))
        halves = grows // LANES
        idrow = []
        for h in range(halves):
            c = g * halves + h
            dcol = d[h * LANES : (h + 1) * LANES]
            dsend[pl.ds(c, 1), :] = jnp.sum(jnp.where(eye, dcol, 0.0), axis=0, keepdims=True)
            idrow.append(ids_v[pl.ds(c, 1), :])
        near = RAMP + d
        term = -RAMP * (1.0 + RAMP) / (near * near) * pcol[at, :]
        hi, lo = split2(term * w)
        both = jnp.concatenate([hi, lo], axis=1)
        idr = jnp.concatenate(idrow, axis=1)
        xid = idr // wy
        yhot = onehot(yrow == idr % wy)

        for q in range(gsrc):
            c = g * (gsrc // 8) + q // 8
            back = row_copy(
                dsend.at[pl.ds(c, 1)], drecv.at[pl.ds(g * gsrc + q, 1)], dsem, drsem, behind(g, q)
            )
            if q:
                back.start()
            else:
                pl.when(g > 0)(back.start)

        pick = jnp.concatenate([jnp.where(xid == x, yhot, 0.0) for x in range(wx)], axis=0)
        added = mm(pick.astype(BF16), both)
        acc[...] = acc[...] + (added[:, :LANES] + added[:, LANES:])

    @pl.loop(0, wx)
    def _(x):
        at = pl.ds(pl.multiple_of(x * wy, wy), wy)
        t = th[at, :]
        ext[x + 2, YO : YO + wy, :] = acc[at, :] * ((SHARP / (2.0 * T0)) * (1.0 - t * t))

    xl, xh = (brick + (nb - 1)) % nb, (brick + 1) % nb
    yl, yh = (dom + (nd - 1)) % nd, (dom + 1) % nd
    ys, y_all = pl.ds(YO, wy), pl.ds(2, wx)
    moves = [
        ((pl.ds(2, 2), ys), (pl.ds(wx + 2, 2), ys), (xl, dom)),
        ((pl.ds(wx, 2), ys), (pl.ds(0, 2), ys), (xh, dom)),
        ((y_all, pl.ds(YO, 2)), (y_all, pl.ds(YO + wy, 2)), (brick, yl)),
        ((y_all, pl.ds(YO + wy - 2, 2)), (y_all, pl.ds(YO - 2, 2)), (brick, yh)),
        ((pl.ds(2, 1), pl.ds(YO, 1)), (pl.ds(wx + 2, 1), pl.ds(YO + wy, 1)), (xl, yl)),
        ((pl.ds(2, 1), pl.ds(YO + wy - 1, 1)), (pl.ds(wx + 2, 1), pl.ds(YO - 1, 1)), (xl, yh)),
        ((pl.ds(wx + 1, 1), pl.ds(YO, 1)), (pl.ds(1, 1), pl.ds(YO + wy, 1)), (xh, yl)),
        ((pl.ds(wx + 1, 1), pl.ds(YO + wy - 1, 1)), (pl.ds(1, 1), pl.ds(YO - 1, 1)), (xh, yh)),
    ]
    halos = [
        pltpu.make_async_remote_copy(
            src_ref=ext.at[s], dst_ref=ext.at[t], send_sem=hsem.at[i], recv_sem=hrsem.at[i],
            device_id=to, device_id_type=MESH,
        )
        for i, (s, t, to) in enumerate(moves)
    ]
    for halo in halos:
        halo.start()

    tall = fst.shape[1]

    def around(ref, x, y0, size):
        y = ref[x, y0 : y0 + size, :]
        zline = iota((size, LANES), 1)
        total = ref[x + 1, y0 : y0 + size, :] + ref[x - 1, y0 : y0 + size, :]
        total = total + ref[x, y0 + 1 : y0 + 1 + size, :] + ref[x, y0 - 1 : y0 - 1 + size, :]
        total = total + jnp.where(zline == 0, 0.0, pltpu.roll(y, 1, axis=1))
        total = total + jnp.where(zline == LANES - 1, 0.0, pltpu.roll(y, LANES - 1, axis=1))
        return y, total

    def first_sweep(x, row, size):
        y, near = around(ext, x, YO - 1 + row, size)
        fst[x, row : row + size, :] = 0.19 * y + 0.135 * near

    def in_steps(start, stop, step, act):
        @pl.loop(0, (stop - start) // step)
        def _(i):
            for u in range(step):
                act(start + i * step + u)

        for x in range(start + (stop - start) // step * step, stop):
            act(x)

    in_steps(3, wx + 1, 8, lambda x: first_sweep(x, 8, wy - 8))
    for halo in halos:
        halo.wait()

    for edge, first_x in ((brick == 0, 0), (brick == nb - 1, wx + 2)):

        @pl.when(edge)
        def _():
            ext[first_x : first_x + 2] = jnp.zeros((2, ext.shape[1], LANES), F32)

    for edge, first_y in ((dom == 0, YO - 2), (dom == nd - 1, YO + wy)):

        @pl.when(edge)
        def _():
            @pl.loop(0, wx + 4)
            def _(x):
                ext[x, first_y : first_y + 2, :] = jnp.zeros((2, LANES), F32)

    def rims(x):
        first_sweep(x, 0, 8)
        first_sweep(x, wy, 8)

    for x in (1, 2, wx + 1, wx + 2):
        first_sweep(x, 0, tall)
    in_steps(3, wx + 1, 8, rims)

    for edge, row in ((dom == 0, 0), (dom == nd - 1, wy + 1)):

        @pl.when(edge)
        def _():
            @pl.loop(1, wx + 3)
            def _(x):
                fst[x, row : row + 1, :] = jnp.zeros((1, LANES), F32)

    for edge, first_x in ((brick == 0, 1), (brick == nb - 1, wx + 2)):

        @pl.when(edge)
        def _():
            fst[first_x] = jnp.zeros((tall, LANES), F32)

    def second_sweep(x):
        y, near = around(fst, x + 2, 1, wy)
        out[x] = 0.1 * y + 0.09 * ext[x + 2, YO : YO + wy, :] + 0.135 * near

    half = wx // 2
    stores = [
        pltpu.make_async_copy(out.at[pl.ds(s * half, half)], res_h.at[pl.ds(s * half, half)], osem.at[s])
        for s in range(2)
    ]
    for s in range(2):
        in_steps(s * half, (s + 1) * half, 8, second_sweep)
        stores[s].start()


    pltpu.make_async_copy(dsend.at[pl.ds(0, 1)], drecv.at[pl.ds(0, 1)], drsem).start()

    pltpu.make_async_copy(drecv, drecv, drsem).wait()
    back = jnp.where(is_id, drecv[...], 0.0).T
    packed = jnp.sum(back.reshape(LANES // CAP, CAP, ndev), axis=0)
    spread = mm(jnp.concatenate([piece for piece in split3(packed)], axis=0), mt[...])
    spread = spread[:CAP] + (spread[CAP : 2 * CAP] + spread[2 * CAP :])
    den[...] = jnp.sum(jnp.where(kmask, spread, 0.0), axis=0, keepdims=True)

    others = pl.ds(1, ndev - 1)
    row_copy(msend.at[others], mrecv.at[others], msem, mrsem, (brick, dom)).wait_send()
    most = pl.ds(CAP, slots - CAP)
    row_copy(send.at[most], recv.at[most], ssem, rsem.at[0], (brick, dom)).wait_send()
    row_copy(drecv.at[others], drecv.at[others], dsem, drsem, (brick, dom)).wait_send()
    for store in stores:
        store.wait()


def body(velocity, adjoint, coupling, jac_weight, owner, local_block, offsets, margin, filtered):
    nb, nd = lax.axis_size("brick"), lax.axis_size("dom")
    ndev = nb * nd
    count = owner.shape[0]
    wx, wy, depth = filtered.shape
    slots = ndev * CAP
    wide = wy + 16
    vmem = pl.BlockSpec(memory_space=pltpu.VMEM)
    hbm = pl.BlockSpec(memory_space=pl.ANY)
    dma = pltpu.SemaphoreType.DMA
    result, density = pl.pallas_call(
        functools.partial(kernel, nb, nd, wx, wy),
        out_shape=(
            jax.ShapeDtypeStruct(filtered.shape, F32),
            jax.ShapeDtypeStruct((1, count), F32),
        ),
        in_specs=[vmem] * 4 + [hbm] * 5,
        out_specs=(hbm, vmem),
        scratch_shapes=[
            pltpu.VMEM(velocity.shape, BF16),
            pltpu.VMEM(adjoint.shape, BF16),
            pltpu.VMEM(offsets.shape, jnp.int32),
            pltpu.VMEM(margin.shape, F32),
            pltpu.VMEM((wx * wy, LANES), F32),
            pltpu.VMEM((ndev, count), BF16),
            pltpu.VMEM((1, count), F32),
            pltpu.VMEM((count, 2 * LANES), BF16),
            pltpu.VMEM((offsets.shape[0], LANES), jnp.int32),
            pltpu.VMEM((LANES // 8, offsets.shape[0], LANES), F32),
            pltpu.VMEM((ndev, LANES), F32),
            pltpu.VMEM((ndev, LANES), F32),
            pltpu.VMEM((slots, LANES), F32),
            pltpu.VMEM((slots, LANES), F32),
            pltpu.VMEM((ndev // 8, LANES), jnp.int32),
            pltpu.SMEM((ndev // 8, LANES), jnp.int32),
            pltpu.VMEM((slots, LANES), F32),
            pltpu.VMEM((slots, LANES), F32),
            pltpu.VMEM((wx * wy, LANES), F32),
            pltpu.VMEM((ndev // 8, LANES), F32),
            pltpu.VMEM((ndev, LANES), F32),
            pltpu.VMEM((wx + 4, wide, LANES), F32),
            pltpu.VMEM((wx + 4, wy + 8, LANES), F32),
            pltpu.VMEM(filtered.shape, F32),
            dma((5,)), dma, dma, dma, dma, dma((nd // 2,)), dma, dma, dma((8,)), dma((8,)), dma((2,)),
        ],
        compiler_params=pltpu.CompilerParams(
            collective_id=0, has_side_effects=True, vmem_limit_bytes=60 * 1024 * 1024
        ),
        name="sensitivity",
    )(
        coupling, jac_weight.reshape(1, count), owner.reshape(1, count),
        local_block.reshape(1, count), velocity, adjoint, offsets, margin,
        filtered.reshape(wx * wy, depth),
    )
    return result, density.reshape(count)


def solution(mesh):
    return jax.shard_map(
        body,
        mesh=mesh,
        in_specs=(
            P(None, None, ("brick", "dom")),
            P(None, None, ("brick", "dom")),
            P(),
            P(("brick", "dom")),
            P(("brick", "dom"), None),
            P(("brick", "dom")),
            P(None, ("brick", "dom")),
            P(None, ("brick", "dom")),
            P("brick", "dom", None),
        ),
        out_specs=(P("brick", "dom", None), P(("brick", "dom"))),
        check_vma=False,
    )
```

```python
import functools
import math

import jax
import jax.numpy as jnp
from jax import lax
from jax.experimental import pallas as pl
from jax.experimental.pallas import tpu as pltpu
from jax.sharding import PartitionSpec as P

MESH = pl.DeviceIdType.MESH
CAP = 16
LANES = 128
SHARP = 8.0
THRESHOLD = 0.5
T0 = math.tanh(SHARP * THRESHOLD)
RAMP = 0.1
F32 = jnp.float32
BF16 = jnp.bfloat16
YO = 8
NT = (((1,), (1,)), ((), ()))
NN = (((1,), (0,)), ((), ()))


def mm(a, b, dims=NN):
    return lax.dot_general(a, b, dims, preferred_element_type=F32)


def iota(shape, dim):
    return lax.broadcasted_iota(jnp.int32, shape, dim)


def onehot(mask):
    return jnp.where(mask, 1.0, 0.0).astype(F32)


def split2(x):
    hi = x.astype(BF16)
    return hi, (x - hi.astype(F32)).astype(BF16)


def split3(x):
    hi = x.astype(BF16)
    rest = x - hi.astype(F32)
    mid = rest.astype(BF16)
    return hi, mid, (rest - mid.astype(F32)).astype(BF16)


def kernel(
    nb, nd, wx, wy, coup_h, jac_h, own_h, loc_h, vel_h, adj_h, off_h, mar_h, fil_h,
    res_h, den,
    coup, jac, own, loc, vel, adj, off, mar, th, mt, pos, wt, fine, parts, msend, mrecv, send, recv, ids_v, ids_s, pcol,
    rows, acc, dsend, drecv, ext, fst, out,
    in_sem, smem_sem, msem, mrsem, ssem, rsem, dsem, drsem, hsem, hrsem, osem,
):
    ndev = nb * nd
    count = own.shape[1]
    blocks = count // LANES
    voxel_rows = wx * wy
    slots = ndev * CAP
    xn, zn, yn = nb // 2, nd // 4, 4
    gsrc = xn * yn
    grows = gsrc * CAP
    groups = 2 * zn
    brick = lax.axis_index("brick")
    dom = lax.axis_index("dom")
    xi, ci, zi, yi = brick // 2, brick % 2, dom // yn, dom % yn

    def ahead(g, m):
        p, q = m // yn, m % yn
        r = p + q + (g & (zn - 1))
        return (
            ((xi + p) & (xn - 1)) * 2 + ((ci + g // zn) & 1),
            ((zi + r) & (zn - 1)) * yn + ((yi + q) & (yn - 1)),
        )

    def behind(g, m):
        p, q = m // yn, m % yn
        r = p + q + (g & (zn - 1))
        return (
            ((xi - p) & (xn - 1)) * 2 + ((ci - g // zn) & 1),
            ((zi - r) & (zn - 1)) * yn + ((yi - q) & (yn - 1)),
        )

    def others_in_turn(act, low, high):
        @pl.loop(0, high - max(low, 1))
        def _(i):
            for m in reversed(range(gsrc)):
                act(high - 1 - i, m)

        if low == 0:
            for m in reversed(range(1, gsrc)):
                act(0, m)

    loads = [
        pltpu.make_async_copy(h, v, in_sem.at[i])
        for i, (h, v) in enumerate((
            (vel_h, vel), (adj_h, adj), (off_h, off), (mar_h, mar), (fil_h, th),
            (coup_h, coup), (jac_h, jac), (loc_h, loc), (own_h, own),
        ))
    ]
    for load in reversed(loads):
        load.start()

    barrier = pltpu.get_barrier_semaphore()

    def greet(g, m):
        pl.semaphore_signal(barrier, inc=1, device_id=ahead(g, m), device_id_type=MESH)

    others_in_turn(greet, 0, groups)

    loads[8].wait()
    owners = own[...]
    obrick, odom = owners // nd, owners % nd
    op = (obrick // 2 - xi) & (xn - 1)
    oq = (odom % yn - yi) & (yn - 1)
    ok = (odom // yn - zi - op - oq) & (zn - 1)
    rel = ((((obrick % 2 - ci) & 1) * zn + ok) * xn + op) * yn + oq
    rr = iota((LANES, 2 * LANES), 0)
    cc = iota((LANES, 2 * LANES), 1)
    upper = onehot((rr < cc) | (cc >= LANES)).astype(BF16)
    hits = [onehot(rel[:, b * LANES : (b + 1) * LANES] == iota((ndev, LANES), 0)) for b in range(blocks)]
    counted = mm(jnp.concatenate(hits, axis=0).astype(BF16), upper)
    base = jnp.zeros((ndev, LANES), F32)
    for b in range(blocks):
        sl = slice(b * LANES, (b + 1) * LANES)
        here = counted[b * ndev : (b + 1) * ndev]
        mt[:, sl] = hits[b].astype(BF16)
        pos[:, sl] = jnp.sum((here[:, :LANES] + base) * hits[b], axis=0, keepdims=True)
        base = base + here[:, LANES:]
    posi = pos[...].astype(jnp.int32)
    placed = rel * CAP + posi

    for load in (*loads[:2], *loads[5:8]):
        load.wait()
    total = None
    for c in range(3):
        part = vel[c].astype(F32) * mm(coup[...], adj[c])
        total = part if total is None else total + part
    product = jac[...] * jnp.sum(total, axis=0, keepdims=True)

    kmask = iota((CAP, count), 0) == posi
    ids = loc[...]
    values = [(ids // 64).astype(F32), (ids % 64).astype(F32)]
    values += [piece.astype(F32) for piece in split3(product)]
    stack = jnp.concatenate([jnp.where(kmask, v, 0.0) for v in values], axis=0).astype(BF16)
    lined = mm(stack, mt[...], NT)
    pieces = [lined[u * CAP : (u + 1) * CAP] for u in range(5)]
    id_rows = jnp.concatenate([64.0 * pieces[0] + pieces[1]] * 8, axis=0).T
    p_rows = jnp.concatenate([pieces[2] + (pieces[3] + pieces[4])] * 8, axis=0).T
    jrow = iota((ndev, LANES), 0) % 8
    jlane = iota((ndev, LANES), 1) // CAP
    is_id = jlane == jrow
    is_p = jlane == (jrow + 4) % 8
    msend[...] = jnp.where(is_id, id_rows, jnp.where(is_p, p_rows, 0.0))

    loads[2].wait()
    loads[3].wait()
    entries = off.shape[0]
    tiles = LANES // 8
    sub = iota((8, LANES), 0)
    for b in range(blocks):
        sl = slice(b * LANES, (b + 1) * LANES)

        @pl.loop(0, entries // 8, unroll=2)
        def _(i):
            at = pl.ds(pl.multiple_of(i * 8, 8), 8)
            o8 = off[at, sl]
            m8 = mar[at, sl]
            fine[at, :] = o8 & 7
            tile = o8 >> 3
            for u in range(tiles):
                parts[u, at, :] = jnp.where(tile == u, m8, 0.0)

        def summed(first):
            def slot8(i, totals):
                totals = list(totals)
                for k in range(8):
                    row = pl.ds(i * 8 + k, 1)
                    hit = jnp.broadcast_to(fine[row, :], (8, LANES)) == sub
                    for u in range(tiles // 2):
                        part = jnp.broadcast_to(parts[first + u, row, :], (8, LANES))
                        totals[u] = totals[u] + jnp.where(hit, part, 0.0)
                return tuple(totals)

            zero = jnp.zeros((8, LANES), F32)
            return lax.fori_loop(0, entries // 8, slot8, (zero,) * (tiles // 2), unroll=2)

        built = jnp.concatenate(summed(0) + summed(tiles // 2), axis=0)
        hi, lo = split2(built.T)
        wt[sl, 0:LANES] = hi
        wt[sl, LANES : 2 * LANES] = lo

    pl.semaphore_wait(barrier, ndev - 1)

    def row_copy(src, dst, send_sem, recv_sem, to):
        return pltpu.make_async_remote_copy(
            src_ref=src, dst_ref=dst, send_sem=send_sem, recv_sem=recv_sem,
            device_id=to, device_id_type=MESH,
        )

    pltpu.make_async_copy(msend.at[pl.ds(0, 1)], mrecv.at[pl.ds(0, 1)], mrsem).start()

    def send_meta(g, m):
        row = pl.ds(g * gsrc + m, 1)
        row_copy(msend.at[row], mrecv.at[row], msem, mrsem, ahead(g, m)).start()

    others_in_turn(send_meta, 0, groups)

    def send_maps(g, m):
        at = pl.ds(pl.multiple_of((g * gsrc + m) * CAP, CAP), CAP)
        row_copy(send.at[at], recv.at[at], ssem, rsem.at[g], ahead(g, m)).start()

    for low, high in ((groups // 2, groups), (0, groups // 2)):
        start, size = low * grows, (high - low) * grows
        pick = onehot(placed == iota((size, count), 0) + start).astype(BF16)
        both = mm(pick, wt[...])
        send[start : start + size, :] = both[:, :LANES] + both[:, LANES:]
        others_in_turn(send_maps, low, high)

    own_rows = pl.ds(0, CAP)
    pltpu.make_async_copy(send.at[own_rows], recv.at[own_rows], rsem.at[0]).start()
    loads[4].wait()

    @pl.loop(0, wx)
    def _(x):
        at = pl.ds(pl.multiple_of(x * wy, wy), wy)
        th[at, :] = jnp.tanh(SHARP * (th[at, :] - THRESHOLD))
        acc[at, :] = jnp.zeros((wy, LANES), F32)

    pltpu.make_async_copy(mrecv, mrecv, mrsem).wait()
    got = mrecv[...]
    chunk_ids = jnp.sum(jnp.where(is_id, got, 0.0).reshape(ndev // 8, 8, LANES), axis=1)
    chunk_p = jnp.sum(jnp.where(is_p, got, 0.0).reshape(ndev // 8, 8, LANES), axis=1)
    p_lines = pltpu.roll(chunk_p, LANES // 2, axis=1)
    ids_v[...] = chunk_ids.astype(jnp.int32)
    to_smem = pltpu.make_async_copy(ids_v, ids_s, smem_sem)
    to_smem.start()
    to_smem.wait()

    eye = iota((LANES, LANES), 0) == iota((LANES, LANES), 1)
    for c in range(ndev // 8):
        line = jnp.sum(jnp.where(eye, p_lines[c : c + 1], 0.0), axis=1, keepdims=True)
        pcol[c * LANES : (c + 1) * LANES, :] = jnp.broadcast_to(line, (LANES, LANES))

    @pl.loop(0, slots // LANES)
    def _(c):
        for k in range(LANES):
            at = ids_s[c, k] & (voxel_rows - 1)
            rows[pl.ds(c * LANES + k, 1), :] = th[pl.ds(at, 1), :]

    yrow = iota((wy, grows), 0)

    @pl.loop(0, groups)
    def _(i):
        g = groups - 1 - i
        at = pl.ds(pl.multiple_of(g * grows, grows), grows)
        pltpu.make_async_copy(recv.at[at], recv.at[at], rsem.at[g]).wait()
        w = recv[at, :]
        d = jnp.sum((rows[at, :] + T0) * w, axis=1, keepdims=True) * (1.0 / (2.0 * T0))
        halves = grows // LANES
        idrow = []
        for h in range(halves):
            c = g * halves + h
            dcol = d[h * LANES : (h + 1) * LANES]
            dsend[pl.ds(c, 1), :] = jnp.sum(jnp.where(eye, dcol, 0.0), axis=0, keepdims=True)
            idrow.append(ids_v[pl.ds(c, 1), :])
        near = RAMP + d
        term = -RAMP * (1.0 + RAMP) / (near * near) * pcol[at, :]
        hi, lo = split2(term * w)
        both = jnp.concatenate([hi, lo], axis=1)
        idr = jnp.concatenate(idrow, axis=1)
        xid = idr // wy
        yhot = onehot(yrow == idr % wy)

        for q in range(gsrc):
            c = g * (gsrc // 8) + q // 8
            back = row_copy(
                dsend.at[pl.ds(c, 1)], drecv.at[pl.ds(g * gsrc + q, 1)], dsem, drsem, behind(g, q)
            )
            if q:
                back.start()
            else:
                pl.when(g > 0)(back.start)

        pick = jnp.concatenate([jnp.where(xid == x, yhot, 0.0) for x in range(wx)], axis=0)
        added = mm(pick.astype(BF16), both)
        acc[...] = acc[...] + (added[:, :LANES] + added[:, LANES:])

    def in_steps(start, stop, step, act):
        @pl.loop(0, (stop - start) // step)
        def _(i):
            for u in range(step):
                act(start + i * step + u)

        for x in range(start + (stop - start) // step * step, stop):
            act(x)

    def source(x, row, size):
        at = pl.ds(pl.multiple_of(x * wy + row, 8), size)
        t = th[at, :]
        ext[x + 2, YO + row : YO + row + size, :] = acc[at, :] * ((SHARP / (2.0 * T0)) * (1.0 - t * t))

    def source_rims(x):
        source(x, 0, 8)
        source(x, wy - 8, 8)

    in_steps(0, wx, 8, source_rims)
    for x in (0, 1, wx - 2, wx - 1):
        source(x, 8, wy - 16)

    xl, xh = (brick + (nb - 1)) % nb, (brick + 1) % nb
    yl, yh = (dom + (nd - 1)) % nd, (dom + 1) % nd
    ys, y_all = pl.ds(YO, wy), pl.ds(2, wx)
    moves = [
        ((pl.ds(2, 2), ys), (pl.ds(wx + 2, 2), ys), (xl, dom)),
        ((pl.ds(wx, 2), ys), (pl.ds(0, 2), ys), (xh, dom)),
        ((y_all, pl.ds(YO, 2)), (y_all, pl.ds(YO + wy, 2)), (brick, yl)),
        ((y_all, pl.ds(YO + wy - 2, 2)), (y_all, pl.ds(YO - 2, 2)), (brick, yh)),
        ((pl.ds(2, 1), pl.ds(YO, 1)), (pl.ds(wx + 2, 1), pl.ds(YO + wy, 1)), (xl, yl)),
        ((pl.ds(2, 1), pl.ds(YO + wy - 1, 1)), (pl.ds(wx + 2, 1), pl.ds(YO - 1, 1)), (xl, yh)),
        ((pl.ds(wx + 1, 1), pl.ds(YO, 1)), (pl.ds(1, 1), pl.ds(YO + wy, 1)), (xh, yl)),
        ((pl.ds(wx + 1, 1), pl.ds(YO + wy - 1, 1)), (pl.ds(1, 1), pl.ds(YO - 1, 1)), (xh, yh)),
    ]
    halos = [
        pltpu.make_async_remote_copy(
            src_ref=ext.at[s], dst_ref=ext.at[t], send_sem=hsem.at[i], recv_sem=hrsem.at[i],
            device_id=to, device_id_type=MESH,
        )
        for i, (s, t, to) in enumerate(moves)
    ]
    for halo in halos:
        halo.start()

    in_steps(2, wx - 2, 6, lambda x: source(x, 8, wy - 16))
    tall = fst.shape[1]

    def around(ref, x, y0, size):
        y = ref[x, y0 : y0 + size, :]
        zline = iota((size, LANES), 1)
        total = ref[x + 1, y0 : y0 + size, :] + ref[x - 1, y0 : y0 + size, :]
        total = total + ref[x, y0 + 1 : y0 + 1 + size, :] + ref[x, y0 - 1 : y0 - 1 + size, :]
        total = total + jnp.where(zline == 0, 0.0, pltpu.roll(y, 1, axis=1))
        total = total + jnp.where(zline == LANES - 1, 0.0, pltpu.roll(y, LANES - 1, axis=1))
        return y, total

    def first_sweep(x, row, size):
        y, near = around(ext, x, YO - 1 + row, size)
        fst[x, row : row + size, :] = 0.19 * y + 0.135 * near

    in_steps(3, wx + 1, 8, lambda x: first_sweep(x, 8, wy - 8))
    for halo in halos:
        halo.wait()

    for edge, first_x in ((brick == 0, 0), (brick == nb - 1, wx + 2)):

        @pl.when(edge)
        def _():
            ext[first_x : first_x + 2] = jnp.zeros((2, ext.shape[1], LANES), F32)

    for edge, first_y in ((dom == 0, YO - 2), (dom == nd - 1, YO + wy)):

        @pl.when(edge)
        def _():
            @pl.loop(0, wx + 4)
            def _(x):
                ext[x, first_y : first_y + 2, :] = jnp.zeros((2, LANES), F32)

    def rims(x):
        first_sweep(x, 0, 8)
        first_sweep(x, wy, 8)

    for x in (1, 2, wx + 1, wx + 2):
        first_sweep(x, 0, tall)
    in_steps(3, wx + 1, 8, rims)

    for edge, row in ((dom == 0, 0), (dom == nd - 1, wy + 1)):

        @pl.when(edge)
        def _():
            @pl.loop(1, wx + 3)
            def _(x):
                fst[x, row : row + 1, :] = jnp.zeros((1, LANES), F32)

    for edge, first_x in ((brick == 0, 1), (brick == nb - 1, wx + 2)):

        @pl.when(edge)
        def _():
            fst[first_x] = jnp.zeros((tall, LANES), F32)

    def second_sweep(x):
        y, near = around(fst, x + 2, 1, wy)
        out[x] = 0.1 * y + 0.09 * ext[x + 2, YO : YO + wy, :] + 0.135 * near

    half = wx // 2
    stores = [
        pltpu.make_async_copy(out.at[pl.ds(s * half, half)], res_h.at[pl.ds(s * half, half)], osem.at[s])
        for s in range(2)
    ]
    for s in range(2):
        in_steps(s * half, (s + 1) * half, 8, second_sweep)
        stores[s].start()


    pltpu.make_async_copy(dsend.at[pl.ds(0, 1)], drecv.at[pl.ds(0, 1)], drsem).start()

    pltpu.make_async_copy(drecv, drecv, drsem).wait()
    back = jnp.where(is_id, drecv[...], 0.0).T
    packed = jnp.sum(back.reshape(LANES // CAP, CAP, ndev), axis=0)
    spread = mm(jnp.concatenate([piece for piece in split3(packed)], axis=0), mt[...])
    spread = spread[:CAP] + (spread[CAP : 2 * CAP] + spread[2 * CAP :])
    den[...] = jnp.sum(jnp.where(kmask, spread, 0.0), axis=0, keepdims=True)

    others = pl.ds(1, ndev - 1)
    row_copy(msend.at[others], mrecv.at[others], msem, mrsem, (brick, dom)).wait_send()
    most = pl.ds(CAP, slots - CAP)
    row_copy(send.at[most], recv.at[most], ssem, rsem.at[0], (brick, dom)).wait_send()
    row_copy(drecv.at[others], drecv.at[others], dsem, drsem, (brick, dom)).wait_send()
    for store in stores:
        store.wait()


def body(velocity, adjoint, coupling, jac_weight, owner, local_block, offsets, margin, filtered):
    nb, nd = lax.axis_size("brick"), lax.axis_size("dom")
    ndev = nb * nd
    count = owner.shape[0]
    wx, wy, depth = filtered.shape
    slots = ndev * CAP
    wide = wy + 16
    vmem = pl.BlockSpec(memory_space=pltpu.VMEM)
    hbm = pl.BlockSpec(memory_space=pl.ANY)
    dma = pltpu.SemaphoreType.DMA
    result, density = pl.pallas_call(
        functools.partial(kernel, nb, nd, wx, wy),
        out_shape=(
            jax.ShapeDtypeStruct(filtered.shape, F32),
            jax.ShapeDtypeStruct((1, count), F32),
        ),
        in_specs=[hbm] * 9,
        out_specs=(hbm, vmem),
        scratch_shapes=[
            pltpu.VMEM(coupling.shape, BF16),
            pltpu.VMEM((1, count), F32),
            pltpu.VMEM((1, count), jnp.int32),
            pltpu.VMEM((1, count), jnp.int32),
            pltpu.VMEM(velocity.shape, BF16),
            pltpu.VMEM(adjoint.shape, BF16),
            pltpu.VMEM(offsets.shape, jnp.int32),
            pltpu.VMEM(margin.shape, F32),
            pltpu.VMEM((wx * wy, LANES), F32),
            pltpu.VMEM((ndev, count), BF16),
            pltpu.VMEM((1, count), F32),
            pltpu.VMEM((count, 2 * LANES), BF16),
            pltpu.VMEM((offsets.shape[0], LANES), jnp.int32),
            pltpu.VMEM((LANES // 8, offsets.shape[0], LANES), F32),
            pltpu.VMEM((ndev, LANES), F32),
            pltpu.VMEM((ndev, LANES), F32),
            pltpu.VMEM((slots, LANES), F32),
            pltpu.VMEM((slots, LANES), F32),
            pltpu.VMEM((ndev // 8, LANES), jnp.int32),
            pltpu.SMEM((ndev // 8, LANES), jnp.int32),
            pltpu.VMEM((slots, LANES), F32),
            pltpu.VMEM((slots, LANES), F32),
            pltpu.VMEM((wx * wy, LANES), F32),
            pltpu.VMEM((ndev // 8, LANES), F32),
            pltpu.VMEM((ndev, LANES), F32),
            pltpu.VMEM((wx + 4, wide, LANES), F32),
            pltpu.VMEM((wx + 4, wy + 8, LANES), F32),
            pltpu.VMEM(filtered.shape, F32),
            dma((9,)), dma, dma, dma, dma, dma((nd // 2,)), dma, dma, dma((8,)), dma((8,)), dma((2,)),
        ],
        compiler_params=pltpu.CompilerParams(
            collective_id=0, has_side_effects=True, vmem_limit_bytes=60 * 1024 * 1024
        ),
        name="sensitivity",
    )(
        coupling, jac_weight.reshape(1, count), owner.reshape(1, count),
        local_block.reshape(1, count), velocity, adjoint, offsets, margin,
        filtered.reshape(wx * wy, depth),
    )
    return result, density.reshape(count)


def solution(mesh):
    return jax.shard_map(
        body,
        mesh=mesh,
        in_specs=(
            P(None, None, ("brick", "dom")),
            P(None, None, ("brick", "dom")),
            P(),
            P(("brick", "dom")),
            P(("brick", "dom"), None),
            P(("brick", "dom")),
            P(None, ("brick", "dom")),
            P(None, ("brick", "dom")),
            P("brick", "dom", None),
        ),
        out_specs=(P("brick", "dom", None), P(("brick", "dom"))),
        check_vma=False,
    )
```

```python
import functools
import math

import jax
import jax.numpy as jnp
from jax import lax
from jax.experimental import pallas as pl
from jax.experimental.pallas import tpu as pltpu
from jax.sharding import PartitionSpec as P

MESH = pl.DeviceIdType.MESH
CAP = 16
LANES = 128
SHARP = 8.0
THRESHOLD = 0.5
T0 = math.tanh(SHARP * THRESHOLD)
RAMP = 0.1
F32 = jnp.float32
BF16 = jnp.bfloat16
YO = 8
NT = (((1,), (1,)), ((), ()))
NN = (((1,), (0,)), ((), ()))


def mm(a, b, dims=NN):
    return lax.dot_general(a, b, dims, preferred_element_type=F32)


def iota(shape, dim):
    return lax.broadcasted_iota(jnp.int32, shape, dim)


def onehot(mask):
    return jnp.where(mask, 1.0, 0.0).astype(F32)


def split2(x):
    hi = x.astype(BF16)
    return hi, (x - hi.astype(F32)).astype(BF16)


def split3(x):
    hi = x.astype(BF16)
    rest = x - hi.astype(F32)
    mid = rest.astype(BF16)
    return hi, mid, (rest - mid.astype(F32)).astype(BF16)


def kernel(
    nb, nd, wx, wy, coup_h, jac_h, own_h, loc_h, vel_h, adj_h, off_h, mar_h, fil_h,
    res_h, den,
    coup, jac, own, loc, vel, adj, off, mar, th, mt, pos, wt, fine, parts, msend, mrecv, send, recv, ids_v, ids_s, pcol,
    rows, acc, dsend, drecv, ext, fst, out,
    in_sem, smem_sem, msem, mrsem, ssem, rsem, dsem, drsem, hsem, hrsem, osem,
):
    ndev = nb * nd
    count = own.shape[1]
    blocks = count // LANES
    voxel_rows = wx * wy
    slots = ndev * CAP
    xn, zn, yn = nb // 2, nd // 4, 4
    gsrc = xn * yn
    grows = gsrc * CAP
    groups = 2 * zn
    brick = lax.axis_index("brick")
    dom = lax.axis_index("dom")
    xi, ci, zi, yi = brick // 2, brick % 2, dom // yn, dom % yn

    def ahead(g, m):
        p, q = m // yn, m % yn
        r = p + q + (g & (zn - 1))
        return (
            ((xi + p) & (xn - 1)) * 2 + ((ci + g // zn) & 1),
            ((zi + r) & (zn - 1)) * yn + ((yi + q) & (yn - 1)),
        )

    def behind(g, m):
        p, q = m // yn, m % yn
        r = p + q + (g & (zn - 1))
        return (
            ((xi - p) & (xn - 1)) * 2 + ((ci - g // zn) & 1),
            ((zi - r) & (zn - 1)) * yn + ((yi - q) & (yn - 1)),
        )

    def others_in_turn(act, low, high):
        @pl.loop(0, high - max(low, 1))
        def _(i):
            for m in reversed(range(gsrc)):
                act(high - 1 - i, m)

        if low == 0:
            for m in reversed(range(1, gsrc)):
                act(0, m)

    loads = [
        pltpu.make_async_copy(h, v, in_sem.at[i])
        for i, (h, v) in enumerate((
            (vel_h, vel), (adj_h, adj), (off_h, off), (mar_h, mar), (fil_h, th),
            (coup_h, coup), (jac_h, jac), (loc_h, loc), (own_h, own),
        ))
    ]
    for load in reversed(loads):
        load.start()

    barrier = pltpu.get_barrier_semaphore()

    def greet(g, m):
        pl.semaphore_signal(barrier, inc=1, device_id=ahead(g, m), device_id_type=MESH)

    others_in_turn(greet, 0, groups)

    loads[8].wait()
    owners = own[...]
    obrick, odom = owners // nd, owners % nd
    op = (obrick // 2 - xi) & (xn - 1)
    oq = (odom % yn - yi) & (yn - 1)
    ok = (odom // yn - zi - op - oq) & (zn - 1)
    rel = ((((obrick % 2 - ci) & 1) * zn + ok) * xn + op) * yn + oq
    rr = iota((LANES, 2 * LANES), 0)
    cc = iota((LANES, 2 * LANES), 1)
    upper = onehot((rr < cc) | (cc >= LANES)).astype(BF16)
    hits = [onehot(rel[:, b * LANES : (b + 1) * LANES] == iota((ndev, LANES), 0)) for b in range(blocks)]
    counted = mm(jnp.concatenate(hits, axis=0).astype(BF16), upper)
    base = jnp.zeros((ndev, LANES), F32)
    for b in range(blocks):
        sl = slice(b * LANES, (b + 1) * LANES)
        here = counted[b * ndev : (b + 1) * ndev]
        mt[:, sl] = hits[b].astype(BF16)
        pos[:, sl] = jnp.sum((here[:, :LANES] + base) * hits[b], axis=0, keepdims=True)
        base = base + here[:, LANES:]
    posi = pos[...].astype(jnp.int32)
    placed = rel * CAP + posi

    loads[2].wait()
    loads[3].wait()
    entries = off.shape[0]
    tiles = LANES // 8
    sub = iota((8, LANES), 0)
    for b in range(blocks):
        sl = slice(b * LANES, (b + 1) * LANES)

        @pl.loop(0, entries // 8, unroll=2)
        def _(i):
            at = pl.ds(pl.multiple_of(i * 8, 8), 8)
            o8 = off[at, sl]
            m8 = mar[at, sl]
            fine[at, :] = o8 & 7
            tile = o8 >> 3
            for u in range(tiles):
                parts[u, at, :] = jnp.where(tile == u, m8, 0.0)

        def summed(first):
            def slot8(i, totals):
                totals = list(totals)
                for k in range(8):
                    row = pl.ds(i * 8 + k, 1)
                    hit = jnp.broadcast_to(fine[row, :], (8, LANES)) == sub
                    for u in range(tiles // 2):
                        part = jnp.broadcast_to(parts[first + u, row, :], (8, LANES))
                        totals[u] = totals[u] + jnp.where(hit, part, 0.0)
                return tuple(totals)

            zero = jnp.zeros((8, LANES), F32)
            return lax.fori_loop(0, entries // 8, slot8, (zero,) * (tiles // 2), unroll=2)

        built = jnp.concatenate(summed(0) + summed(tiles // 2), axis=0)
        hi, lo = split2(built.T)
        wt[sl, 0:LANES] = hi
        wt[sl, LANES : 2 * LANES] = lo

    pl.semaphore_wait(barrier, ndev - 1)

    def row_copy(src, dst, send_sem, recv_sem, to):
        return pltpu.make_async_remote_copy(
            src_ref=src, dst_ref=dst, send_sem=send_sem, recv_sem=recv_sem,
            device_id=to, device_id_type=MESH,
        )

    def send_maps(g, m):
        at = pl.ds(pl.multiple_of((g * gsrc + m) * CAP, CAP), CAP)
        row_copy(send.at[at], recv.at[at], ssem, rsem.at[g], ahead(g, m)).start()

    def place_and_send(low, high):
        start, size = low * grows, (high - low) * grows
        pick = onehot(placed == iota((size, count), 0) + start).astype(BF16)
        both = mm(pick, wt[...])
        send[start : start + size, :] = both[:, :LANES] + both[:, LANES:]
        others_in_turn(send_maps, low, high)

    place_and_send(groups // 2, groups)

    for load in (*loads[:2], *loads[5:8]):
        load.wait()
    total = None
    for c in range(3):
        part = vel[c].astype(F32) * mm(coup[...], adj[c])
        total = part if total is None else total + part
    product = jac[...] * jnp.sum(total, axis=0, keepdims=True)

    kmask = iota((CAP, count), 0) == posi
    ids = loc[...]
    values = [(ids // 64).astype(F32), (ids % 64).astype(F32)]
    values += [piece.astype(F32) for piece in split3(product)]
    stack = jnp.concatenate([jnp.where(kmask, v, 0.0) for v in values], axis=0).astype(BF16)
    lined = mm(stack, mt[...], NT)
    pieces = [lined[u * CAP : (u + 1) * CAP] for u in range(5)]
    id_rows = jnp.concatenate([64.0 * pieces[0] + pieces[1]] * 8, axis=0).T
    p_rows = jnp.concatenate([pieces[2] + (pieces[3] + pieces[4])] * 8, axis=0).T
    jrow = iota((ndev, LANES), 0) % 8
    jlane = iota((ndev, LANES), 1) // CAP
    is_id = jlane == jrow
    is_p = jlane == (jrow + 4) % 8
    msend[...] = jnp.where(is_id, id_rows, jnp.where(is_p, p_rows, 0.0))

    pltpu.make_async_copy(msend.at[pl.ds(0, 1)], mrecv.at[pl.ds(0, 1)], mrsem).start()

    def send_meta(g, m):
        row = pl.ds(g * gsrc + m, 1)
        row_copy(msend.at[row], mrecv.at[row], msem, mrsem, ahead(g, m)).start()

    others_in_turn(send_meta, 0, groups)

    place_and_send(0, groups // 2)

    own_rows = pl.ds(0, CAP)
    pltpu.make_async_copy(send.at[own_rows], recv.at[own_rows], rsem.at[0]).start()
    loads[4].wait()

    @pl.loop(0, wx)
    def _(x):
        at = pl.ds(pl.multiple_of(x * wy, wy), wy)
        th[at, :] = jnp.tanh(SHARP * (th[at, :] - THRESHOLD))
        acc[at, :] = jnp.zeros((wy, LANES), F32)

    pltpu.make_async_copy(mrecv, mrecv, mrsem).wait()
    got = mrecv[...]
    chunk_ids = jnp.sum(jnp.where(is_id, got, 0.0).reshape(ndev // 8, 8, LANES), axis=1)
    chunk_p = jnp.sum(jnp.where(is_p, got, 0.0).reshape(ndev // 8, 8, LANES), axis=1)
    p_lines = pltpu.roll(chunk_p, LANES // 2, axis=1)
    ids_v[...] = chunk_ids.astype(jnp.int32)
    to_smem = pltpu.make_async_copy(ids_v, ids_s, smem_sem)
    to_smem.start()
    to_smem.wait()

    eye = iota((LANES, LANES), 0) == iota((LANES, LANES), 1)
    for c in range(ndev // 8):
        line = jnp.sum(jnp.where(eye, p_lines[c : c + 1], 0.0), axis=1, keepdims=True)
        pcol[c * LANES : (c + 1) * LANES, :] = jnp.broadcast_to(line, (LANES, LANES))

    @pl.loop(0, slots // LANES)
    def _(c):
        for k in range(LANES):
            at = ids_s[c, k] & (voxel_rows - 1)
            rows[pl.ds(c * LANES + k, 1), :] = th[pl.ds(at, 1), :]

    yrow = iota((wy, grows), 0)

    @pl.loop(0, groups)
    def _(i):
        g = groups - 1 - i
        at = pl.ds(pl.multiple_of(g * grows, grows), grows)
        pltpu.make_async_copy(recv.at[at], recv.at[at], rsem.at[g]).wait()
        w = recv[at, :]
        d = jnp.sum((rows[at, :] + T0) * w, axis=1, keepdims=True) * (1.0 / (2.0 * T0))
        halves = grows // LANES
        idrow = []
        for h in range(halves):
            c = g * halves + h
            dcol = d[h * LANES : (h + 1) * LANES]
            dsend[pl.ds(c, 1), :] = jnp.sum(jnp.where(eye, dcol, 0.0), axis=0, keepdims=True)
            idrow.append(ids_v[pl.ds(c, 1), :])
        near = RAMP + d
        term = -RAMP * (1.0 + RAMP) / (near * near) * pcol[at, :]
        hi, lo = split2(term * w)
        both = jnp.concatenate([hi, lo], axis=1)
        idr = jnp.concatenate(idrow, axis=1)
        xid = idr // wy
        yhot = onehot(yrow == idr % wy)

        def reply(q):
            c = g * (gsrc // 8) + q // 8
            row_copy(
                dsend.at[pl.ds(c, 1)], drecv.at[pl.ds(g * gsrc + q, 1)], dsem, drsem, behind(g, q)
            ).start()

        for q in range(1, gsrc):
            reply(q)

        pick = jnp.concatenate([jnp.where(xid == x, yhot, 0.0) for x in range(wx)], axis=0)
        added = mm(pick.astype(BF16), both)
        acc[...] = acc[...] + (added[:, :LANES] + added[:, LANES:])
        pl.when(g > 0)(lambda: reply(0))

    def in_steps(start, stop, step, act):
        @pl.loop(0, (stop - start) // step)
        def _(i):
            for u in range(step):
                act(start + i * step + u)

        for x in range(start + (stop - start) // step * step, stop):
            act(x)

    def source(x, row, size):
        at = pl.ds(pl.multiple_of(x * wy + row, 8), size)
        t = th[at, :]
        ext[x + 2, YO + row : YO + row + size, :] = acc[at, :] * ((SHARP / (2.0 * T0)) * (1.0 - t * t))

    def source_rims(x):
        source(x, 0, 8)
        source(x, wy - 8, 8)

    in_steps(0, wx, 8, source_rims)
    for x in (0, 1, wx - 2, wx - 1):
        source(x, 8, wy - 16)

    xl, xh = (brick + (nb - 1)) % nb, (brick + 1) % nb
    yl, yh = (dom + (nd - 1)) % nd, (dom + 1) % nd
    ys, y_all = pl.ds(YO, wy), pl.ds(2, wx)
    moves = [
        ((pl.ds(2, 2), ys), (pl.ds(wx + 2, 2), ys), (xl, dom)),
        ((pl.ds(wx, 2), ys), (pl.ds(0, 2), ys), (xh, dom)),
        ((y_all, pl.ds(YO, 2)), (y_all, pl.ds(YO + wy, 2)), (brick, yl)),
        ((y_all, pl.ds(YO + wy - 2, 2)), (y_all, pl.ds(YO - 2, 2)), (brick, yh)),
        ((pl.ds(2, 1), pl.ds(YO, 1)), (pl.ds(wx + 2, 1), pl.ds(YO + wy, 1)), (xl, yl)),
        ((pl.ds(2, 1), pl.ds(YO + wy - 1, 1)), (pl.ds(wx + 2, 1), pl.ds(YO - 1, 1)), (xl, yh)),
        ((pl.ds(wx + 1, 1), pl.ds(YO, 1)), (pl.ds(1, 1), pl.ds(YO + wy, 1)), (xh, yl)),
        ((pl.ds(wx + 1, 1), pl.ds(YO + wy - 1, 1)), (pl.ds(1, 1), pl.ds(YO - 1, 1)), (xh, yh)),
    ]
    halos = [
        pltpu.make_async_remote_copy(
            src_ref=ext.at[s], dst_ref=ext.at[t], send_sem=hsem.at[i], recv_sem=hrsem.at[i],
            device_id=to, device_id_type=MESH,
        )
        for i, (s, t, to) in enumerate(moves)
    ]
    for halo in halos:
        halo.start()

    in_steps(2, wx - 2, 6, lambda x: source(x, 8, wy - 16))
    tall = fst.shape[1]

    def around(ref, x, y0, size):
        y = ref[x, y0 : y0 + size, :]
        zline = iota((size, LANES), 1)
        total = ref[x + 1, y0 : y0 + size, :] + ref[x - 1, y0 : y0 + size, :]
        total = total + ref[x, y0 + 1 : y0 + 1 + size, :] + ref[x, y0 - 1 : y0 - 1 + size, :]
        total = total + jnp.where(zline == 0, 0.0, pltpu.roll(y, 1, axis=1))
        total = total + jnp.where(zline == LANES - 1, 0.0, pltpu.roll(y, LANES - 1, axis=1))
        return y, total

    def first_sweep(x, row, size):
        y, near = around(ext, x, YO - 1 + row, size)
        fst[x, row : row + size, :] = 0.19 * y + 0.135 * near

    in_steps(3, wx + 1, 8, lambda x: first_sweep(x, 8, wy - 8))
    for halo in halos:
        halo.wait()

    for edge, first_x in ((brick == 0, 0), (brick == nb - 1, wx + 2)):

        @pl.when(edge)
        def _():
            ext[first_x : first_x + 2] = jnp.zeros((2, ext.shape[1], LANES), F32)

    for edge, first_y in ((dom == 0, YO - 2), (dom == nd - 1, YO + wy)):

        @pl.when(edge)
        def _():
            @pl.loop(0, wx + 4)
            def _(x):
                ext[x, first_y : first_y + 2, :] = jnp.zeros((2, LANES), F32)

    def rims(x):
        first_sweep(x, 0, 8)
        first_sweep(x, wy, 8)

    for x in (1, 2, wx + 1, wx + 2):
        first_sweep(x, 0, tall)
    in_steps(3, wx + 1, 8, rims)

    for edge, row in ((dom == 0, 0), (dom == nd - 1, wy + 1)):

        @pl.when(edge)
        def _():
            @pl.loop(1, wx + 3)
            def _(x):
                fst[x, row : row + 1, :] = jnp.zeros((1, LANES), F32)

    for edge, first_x in ((brick == 0, 1), (brick == nb - 1, wx + 2)):

        @pl.when(edge)
        def _():
            fst[first_x] = jnp.zeros((tall, LANES), F32)

    def second_sweep(x):
        y, near = around(fst, x + 2, 1, wy)
        out[x] = 0.1 * y + 0.09 * ext[x + 2, YO : YO + wy, :] + 0.135 * near

    half = wx // 2
    stores = [
        pltpu.make_async_copy(out.at[pl.ds(s * half, half)], res_h.at[pl.ds(s * half, half)], osem.at[s])
        for s in range(2)
    ]
    for s in range(2):
        in_steps(s * half, (s + 1) * half, 8, second_sweep)
        stores[s].start()


    pltpu.make_async_copy(dsend.at[pl.ds(0, 1)], drecv.at[pl.ds(0, 1)], drsem).start()

    pltpu.make_async_copy(drecv, drecv, drsem).wait()
    back = jnp.where(is_id, drecv[...], 0.0).T
    packed = jnp.sum(back.reshape(LANES // CAP, CAP, ndev), axis=0)
    spread = mm(jnp.concatenate([piece for piece in split3(packed)], axis=0), mt[...])
    spread = spread[:CAP] + (spread[CAP : 2 * CAP] + spread[2 * CAP :])
    den[...] = jnp.sum(jnp.where(kmask, spread, 0.0), axis=0, keepdims=True)

    others = pl.ds(1, ndev - 1)
    row_copy(msend.at[others], mrecv.at[others], msem, mrsem, (brick, dom)).wait_send()
    most = pl.ds(CAP, slots - CAP)
    row_copy(send.at[most], recv.at[most], ssem, rsem.at[0], (brick, dom)).wait_send()
    row_copy(drecv.at[others], drecv.at[others], dsem, drsem, (brick, dom)).wait_send()
    for store in stores:
        store.wait()


def body(velocity, adjoint, coupling, jac_weight, owner, local_block, offsets, margin, filtered):
    nb, nd = lax.axis_size("brick"), lax.axis_size("dom")
    ndev = nb * nd
    count = owner.shape[0]
    wx, wy, depth = filtered.shape
    slots = ndev * CAP
    wide = wy + 16
    vmem = pl.BlockSpec(memory_space=pltpu.VMEM)
    hbm = pl.BlockSpec(memory_space=pl.ANY)
    dma = pltpu.SemaphoreType.DMA
    result, density = pl.pallas_call(
        functools.partial(kernel, nb, nd, wx, wy),
        out_shape=(
            jax.ShapeDtypeStruct(filtered.shape, F32),
            jax.ShapeDtypeStruct((1, count), F32),
        ),
        in_specs=[hbm] * 9,
        out_specs=(hbm, vmem),
        scratch_shapes=[
            pltpu.VMEM(coupling.shape, BF16),
            pltpu.VMEM((1, count), F32),
            pltpu.VMEM((1, count), jnp.int32),
            pltpu.VMEM((1, count), jnp.int32),
            pltpu.VMEM(velocity.shape, BF16),
            pltpu.VMEM(adjoint.shape, BF16),
            pltpu.VMEM(offsets.shape, jnp.int32),
            pltpu.VMEM(margin.shape, F32),
            pltpu.VMEM((wx * wy, LANES), F32),
            pltpu.VMEM((ndev, count), BF16),
            pltpu.VMEM((1, count), F32),
            pltpu.VMEM((count, 2 * LANES), BF16),
            pltpu.VMEM((offsets.shape[0], LANES), jnp.int32),
            pltpu.VMEM((LANES // 8, offsets.shape[0], LANES), F32),
            pltpu.VMEM((ndev, LANES), F32),
            pltpu.VMEM((ndev, LANES), F32),
            pltpu.VMEM((slots, LANES), F32),
            pltpu.VMEM((slots, LANES), F32),
            pltpu.VMEM((ndev // 8, LANES), jnp.int32),
            pltpu.SMEM((ndev // 8, LANES), jnp.int32),
            pltpu.VMEM((slots, LANES), F32),
            pltpu.VMEM((slots, LANES), F32),
            pltpu.VMEM((wx * wy, LANES), F32),
            pltpu.VMEM((ndev // 8, LANES), F32),
            pltpu.VMEM((ndev, LANES), F32),
            pltpu.VMEM((wx + 4, wide, LANES), F32),
            pltpu.VMEM((wx + 4, wy + 8, LANES), F32),
            pltpu.VMEM(filtered.shape, F32),
            dma((9,)), dma, dma, dma, dma, dma((nd // 2,)), dma, dma, dma((8,)), dma((8,)), dma((2,)),
        ],
        compiler_params=pltpu.CompilerParams(
            collective_id=0, has_side_effects=True, vmem_limit_bytes=60 * 1024 * 1024
        ),
        name="sensitivity",
    )(
        coupling, jac_weight.reshape(1, count), owner.reshape(1, count),
        local_block.reshape(1, count), velocity, adjoint, offsets, margin,
        filtered.reshape(wx * wy, depth),
    )
    return result, density.reshape(count)


def solution(mesh):
    return jax.shard_map(
        body,
        mesh=mesh,
        in_specs=(
            P(None, None, ("brick", "dom")),
            P(None, None, ("brick", "dom")),
            P(),
            P(("brick", "dom")),
            P(("brick", "dom"), None),
            P(("brick", "dom")),
            P(None, ("brick", "dom")),
            P(None, ("brick", "dom")),
            P("brick", "dom", None),
        ),
        out_specs=(P("brick", "dom", None), P(("brick", "dom"))),
        check_vma=False,
    )
```

```python
import functools
import math

import jax
import jax.numpy as jnp
from jax import lax
from jax.experimental import pallas as pl
from jax.experimental.pallas import tpu as pltpu
from jax.sharding import PartitionSpec as P

MESH = pl.DeviceIdType.MESH
CAP = 16
LANES = 128
SHARP = 8.0
THRESHOLD = 0.5
T0 = math.tanh(SHARP * THRESHOLD)
RAMP = 0.1
F32 = jnp.float32
BF16 = jnp.bfloat16
YO = 8
NT = (((1,), (1,)), ((), ()))
NN = (((1,), (0,)), ((), ()))


def mm(a, b, dims=NN):
    return lax.dot_general(a, b, dims, preferred_element_type=F32)


def iota(shape, dim):
    return lax.broadcasted_iota(jnp.int32, shape, dim)


def onehot(mask):
    return jnp.where(mask, 1.0, 0.0).astype(F32)


def split2(x):
    hi = x.astype(BF16)
    return hi, (x - hi.astype(F32)).astype(BF16)


def split3(x):
    hi = x.astype(BF16)
    rest = x - hi.astype(F32)
    mid = rest.astype(BF16)
    return hi, mid, (rest - mid.astype(F32)).astype(BF16)


def kernel(
    nb, nd, wx, wy, coup_h, jac_h, own_h, loc_h, vel_h, adj_h, off_h, mar_h, fil_h,
    res_h, den,
    coup, jac, own, loc, vel, adj, off, mar, th, mt, pos, wt, fine, parts, msend, mrecv, send, recv, ids_v, ids_s, pcol,
    rows, acc, dsend, drecv, ext, fst, out,
    in_sem, smem_sem, msem, mrsem, ssem, rsem, dsem, drsem, hsem, hrsem, osem,
):
    ndev = nb * nd
    count = own.shape[1]
    blocks = count // LANES
    voxel_rows = wx * wy
    slots = ndev * CAP
    xn, zn, yn = nb // 2, nd // 4, 4
    gsrc = xn * yn
    grows = gsrc * CAP
    groups = 2 * zn
    brick = lax.axis_index("brick")
    dom = lax.axis_index("dom")
    xi, ci, zi, yi = brick // 2, brick % 2, dom // yn, dom % yn

    def ahead(g, m):
        p, q = m // yn, m % yn
        r = p + q + (g & (zn - 1))
        return (
            ((xi + p) & (xn - 1)) * 2 + ((ci + g // zn) & 1),
            ((zi + r) & (zn - 1)) * yn + ((yi + q) & (yn - 1)),
        )

    def behind(g, m):
        p, q = m // yn, m % yn
        r = p + q + (g & (zn - 1))
        return (
            ((xi - p) & (xn - 1)) * 2 + ((ci - g // zn) & 1),
            ((zi - r) & (zn - 1)) * yn + ((yi - q) & (yn - 1)),
        )

    def others_in_turn(act, low, high):
        @pl.loop(0, high - max(low, 1))
        def _(i):
            for m in reversed(range(gsrc)):
                act(high - 1 - i, m)

        if low == 0:
            for m in reversed(range(1, gsrc)):
                act(0, m)

    loads = [
        pltpu.make_async_copy(h, v, in_sem.at[i])
        for i, (h, v) in enumerate((
            (vel_h, vel), (adj_h, adj), (off_h, off), (mar_h, mar), (fil_h, th),
            (coup_h, coup), (jac_h, jac), (loc_h, loc), (own_h, own),
        ))
    ]
    for load in reversed(loads):
        load.start()

    barrier = pltpu.get_barrier_semaphore()

    def greet(g, m):
        pl.semaphore_signal(barrier, inc=1, device_id=ahead(g, m), device_id_type=MESH)

    others_in_turn(greet, 0, groups)

    loads[8].wait()
    owners = own[...]
    obrick, odom = owners // nd, owners % nd
    op = (obrick // 2 - xi) & (xn - 1)
    oq = (odom % yn - yi) & (yn - 1)
    ok = (odom // yn - zi - op - oq) & (zn - 1)
    rel = ((((obrick % 2 - ci) & 1) * zn + ok) * xn + op) * yn + oq
    rr = iota((LANES, 2 * LANES), 0)
    cc = iota((LANES, 2 * LANES), 1)
    upper = onehot((rr < cc) | (cc >= LANES)).astype(BF16)
    hits = [onehot(rel[:, b * LANES : (b + 1) * LANES] == iota((ndev, LANES), 0)) for b in range(blocks)]
    counted = mm(jnp.concatenate(hits, axis=0).astype(BF16), upper)
    base = jnp.zeros((ndev, LANES), F32)
    for b in range(blocks):
        sl = slice(b * LANES, (b + 1) * LANES)
        here = counted[b * ndev : (b + 1) * ndev]
        mt[:, sl] = hits[b].astype(BF16)
        pos[:, sl] = jnp.sum((here[:, :LANES] + base) * hits[b], axis=0, keepdims=True)
        base = base + here[:, LANES:]
    posi = pos[...].astype(jnp.int32)
    placed = rel * CAP + posi

    for load in (*loads[:2], *loads[5:8]):
        load.wait()
    total = None
    for c in range(3):
        part = vel[c].astype(F32) * mm(coup[...], adj[c])
        total = part if total is None else total + part
    product = jac[...] * jnp.sum(total, axis=0, keepdims=True)

    kmask = iota((CAP, count), 0) == posi
    ids = loc[...]
    values = [(ids // 64).astype(F32), (ids % 64).astype(F32)]
    values += [piece.astype(F32) for piece in split3(product)]
    stack = jnp.concatenate([jnp.where(kmask, v, 0.0) for v in values], axis=0).astype(BF16)
    lined = mm(stack, mt[...], NT)
    pieces = [lined[u * CAP : (u + 1) * CAP] for u in range(5)]
    id_rows = jnp.concatenate([64.0 * pieces[0] + pieces[1]] * 8, axis=0).T
    p_rows = jnp.concatenate([pieces[2] + (pieces[3] + pieces[4])] * 8, axis=0).T
    jrow = iota((ndev, LANES), 0) % 8
    jlane = iota((ndev, LANES), 1) // CAP
    is_id = jlane == jrow
    is_p = jlane == (jrow + 4) % 8
    msend[...] = jnp.where(is_id, id_rows, jnp.where(is_p, p_rows, 0.0))

    def row_copy(src, dst, send_sem, recv_sem, to):
        return pltpu.make_async_remote_copy(
            src_ref=src, dst_ref=dst, send_sem=send_sem, recv_sem=recv_sem,
            device_id=to, device_id_type=MESH,
        )

    def greeted_and_told():
        pl.semaphore_wait(barrier, ndev - 1)

        pltpu.make_async_copy(msend.at[pl.ds(0, 1)], mrecv.at[pl.ds(0, 1)], mrsem).start()

        def send_meta(g, m):
            row = pl.ds(g * gsrc + m, 1)
            row_copy(msend.at[row], mrecv.at[row], msem, mrsem, ahead(g, m)).start()

        others_in_turn(send_meta, 0, groups)

    loads[2].wait()
    loads[3].wait()
    entries = off.shape[0]
    tiles = LANES // 8
    sub = iota((8, LANES), 0)
    for b in range(blocks):
        sl = slice(b * LANES, (b + 1) * LANES)
        if b == blocks - 2:
            greeted_and_told()

        @pl.loop(0, entries // 8, unroll=2)
        def _(i):
            at = pl.ds(pl.multiple_of(i * 8, 8), 8)
            o8 = off[at, sl]
            m8 = mar[at, sl]
            fine[at, :] = o8 & 7
            tile = o8 >> 3
            for u in range(tiles):
                parts[u, at, :] = jnp.where(tile == u, m8, 0.0)

        def summed(first):
            def slot8(i, totals):
                totals = list(totals)
                for k in range(8):
                    row = pl.ds(i * 8 + k, 1)
                    hit = jnp.broadcast_to(fine[row, :], (8, LANES)) == sub
                    for u in range(tiles // 2):
                        part = jnp.broadcast_to(parts[first + u, row, :], (8, LANES))
                        totals[u] = totals[u] + jnp.where(hit, part, 0.0)
                return tuple(totals)

            zero = jnp.zeros((8, LANES), F32)
            return lax.fori_loop(0, entries // 8, slot8, (zero,) * (tiles // 2), unroll=2)

        built = jnp.concatenate(summed(0) + summed(tiles // 2), axis=0)
        hi, lo = split2(built.T)
        wt[sl, 0:LANES] = hi
        wt[sl, LANES : 2 * LANES] = lo

    def send_maps(g, m):
        at = pl.ds(pl.multiple_of((g * gsrc + m) * CAP, CAP), CAP)
        row_copy(send.at[at], recv.at[at], ssem, rsem.at[g], ahead(g, m)).start()

    for low, high in ((groups // 2, groups), (0, groups // 2)):
        start, size = low * grows, (high - low) * grows
        pick = onehot(placed == iota((size, count), 0) + start).astype(BF16)
        both = mm(pick, wt[...])
        send[start : start + size, :] = both[:, :LANES] + both[:, LANES:]
        others_in_turn(send_maps, low, high)

    own_rows = pl.ds(0, CAP)
    pltpu.make_async_copy(send.at[own_rows], recv.at[own_rows], rsem.at[0]).start()
    loads[4].wait()

    @pl.loop(0, wx)
    def _(x):
        at = pl.ds(pl.multiple_of(x * wy, wy), wy)
        th[at, :] = jnp.tanh(SHARP * (th[at, :] - THRESHOLD))
        acc[at, :] = jnp.zeros((wy, LANES), F32)

    pltpu.make_async_copy(mrecv, mrecv, mrsem).wait()
    got = mrecv[...]
    chunk_ids = jnp.sum(jnp.where(is_id, got, 0.0).reshape(ndev // 8, 8, LANES), axis=1)
    chunk_p = jnp.sum(jnp.where(is_p, got, 0.0).reshape(ndev // 8, 8, LANES), axis=1)
    p_lines = pltpu.roll(chunk_p, LANES // 2, axis=1)
    ids_v[...] = chunk_ids.astype(jnp.int32)
    to_smem = pltpu.make_async_copy(ids_v, ids_s, smem_sem)
    to_smem.start()
    to_smem.wait()

    eye = iota((LANES, LANES), 0) == iota((LANES, LANES), 1)
    for c in range(ndev // 8):
        line = jnp.sum(jnp.where(eye, p_lines[c : c + 1], 0.0), axis=1, keepdims=True)
        pcol[c * LANES : (c + 1) * LANES, :] = jnp.broadcast_to(line, (LANES, LANES))

    @pl.loop(0, slots // LANES)
    def _(c):
        for k in range(LANES):
            at = ids_s[c, k] & (voxel_rows - 1)
            rows[pl.ds(c * LANES + k, 1), :] = th[pl.ds(at, 1), :]

    yrow = iota((wy, grows), 0)

    @pl.loop(0, groups)
    def _(i):
        g = groups - 1 - i
        at = pl.ds(pl.multiple_of(g * grows, grows), grows)
        pltpu.make_async_copy(recv.at[at], recv.at[at], rsem.at[g]).wait()
        w = recv[at, :]
        d = jnp.sum((rows[at, :] + T0) * w, axis=1, keepdims=True) * (1.0 / (2.0 * T0))
        halves = grows // LANES
        idrow = []
        for h in range(halves):
            c = g * halves + h
            dcol = d[h * LANES : (h + 1) * LANES]
            dsend[pl.ds(c, 1), :] = jnp.sum(jnp.where(eye, dcol, 0.0), axis=0, keepdims=True)
            idrow.append(ids_v[pl.ds(c, 1), :])
        near = RAMP + d
        term = -RAMP * (1.0 + RAMP) / (near * near) * pcol[at, :]
        hi, lo = split2(term * w)
        both = jnp.concatenate([hi, lo], axis=1)
        idr = jnp.concatenate(idrow, axis=1)
        xid = idr // wy
        yhot = onehot(yrow == idr % wy)

        for q in range(gsrc):
            c = g * (gsrc // 8) + q // 8
            back = row_copy(
                dsend.at[pl.ds(c, 1)], drecv.at[pl.ds(g * gsrc + q, 1)], dsem, drsem, behind(g, q)
            )
            if q:
                back.start()
            else:
                pl.when(g > 0)(back.start)

        pick = jnp.concatenate([jnp.where(xid == x, yhot, 0.0) for x in range(wx)], axis=0)
        added = mm(pick.astype(BF16), both)
        acc[...] = acc[...] + (added[:, :LANES] + added[:, LANES:])

    def in_steps(start, stop, step, act):
        @pl.loop(0, (stop - start) // step)
        def _(i):
            for u in range(step):
                act(start + i * step + u)

        for x in range(start + (stop - start) // step * step, stop):
            act(x)

    def source(x, row, size):
        at = pl.ds(pl.multiple_of(x * wy + row, 8), size)
        t = th[at, :]
        ext[x + 2, YO + row : YO + row + size, :] = acc[at, :] * ((SHARP / (2.0 * T0)) * (1.0 - t * t))

    def source_rims(x):
        source(x, 0, 8)
        source(x, wy - 8, 8)

    in_steps(0, wx, 8, source_rims)
    for x in (0, 1, wx - 2, wx - 1):
        source(x, 8, wy - 16)

    xl, xh = (brick + (nb - 1)) % nb, (brick + 1) % nb
    yl, yh = (dom + (nd - 1)) % nd, (dom + 1) % nd
    ys, y_all = pl.ds(YO, wy), pl.ds(2, wx)
    moves = [
        ((pl.ds(2, 2), ys), (pl.ds(wx + 2, 2), ys), (xl, dom)),
        ((pl.ds(wx, 2), ys), (pl.ds(0, 2), ys), (xh, dom)),
        ((y_all, pl.ds(YO, 2)), (y_all, pl.ds(YO + wy, 2)), (brick, yl)),
        ((y_all, pl.ds(YO + wy - 2, 2)), (y_all, pl.ds(YO - 2, 2)), (brick, yh)),
        ((pl.ds(2, 1), pl.ds(YO, 1)), (pl.ds(wx + 2, 1), pl.ds(YO + wy, 1)), (xl, yl)),
        ((pl.ds(2, 1), pl.ds(YO + wy - 1, 1)), (pl.ds(wx + 2, 1), pl.ds(YO - 1, 1)), (xl, yh)),
        ((pl.ds(wx + 1, 1), pl.ds(YO, 1)), (pl.ds(1, 1), pl.ds(YO + wy, 1)), (xh, yl)),
        ((pl.ds(wx + 1, 1), pl.ds(YO + wy - 1, 1)), (pl.ds(1, 1), pl.ds(YO - 1, 1)), (xh, yh)),
    ]
    halos = [
        pltpu.make_async_remote_copy(
            src_ref=ext.at[s], dst_ref=ext.at[t], send_sem=hsem.at[i], recv_sem=hrsem.at[i],
            device_id=to, device_id_type=MESH,
        )
        for i, (s, t, to) in enumerate(moves)
    ]
    for halo in halos:
        halo.start()

    in_steps(2, wx - 2, 6, lambda x: source(x, 8, wy - 16))
    tall = fst.shape[1]

    def around(ref, x, y0, size):
        y = ref[x, y0 : y0 + size, :]
        zline = iota((size, LANES), 1)
        total = ref[x + 1, y0 : y0 + size, :] + ref[x - 1, y0 : y0 + size, :]
        total = total + ref[x, y0 + 1 : y0 + 1 + size, :] + ref[x, y0 - 1 : y0 - 1 + size, :]
        total = total + jnp.where(zline == 0, 0.0, pltpu.roll(y, 1, axis=1))
        total = total + jnp.where(zline == LANES - 1, 0.0, pltpu.roll(y, LANES - 1, axis=1))
        return y, total

    def first_sweep(x, row, size):
        y, near = around(ext, x, YO - 1 + row, size)
        fst[x, row : row + size, :] = 0.19 * y + 0.135 * near

    in_steps(3, wx + 1, 8, lambda x: first_sweep(x, 8, wy - 8))
    for halo in halos:
        halo.wait()

    for edge, first_x in ((brick == 0, 0), (brick == nb - 1, wx + 2)):

        @pl.when(edge)
        def _():
            ext[first_x : first_x + 2] = jnp.zeros((2, ext.shape[1], LANES), F32)

    for edge, first_y in ((dom == 0, YO - 2), (dom == nd - 1, YO + wy)):

        @pl.when(edge)
        def _():
            @pl.loop(0, wx + 4)
            def _(x):
                ext[x, first_y : first_y + 2, :] = jnp.zeros((2, LANES), F32)

    def rims(x):
        first_sweep(x, 0, 8)
        first_sweep(x, wy, 8)

    for x in (1, 2, wx + 1, wx + 2):
        first_sweep(x, 0, tall)
    in_steps(3, wx + 1, 8, rims)

    for edge, row in ((dom == 0, 0), (dom == nd - 1, wy + 1)):

        @pl.when(edge)
        def _():
            @pl.loop(1, wx + 3)
            def _(x):
                fst[x, row : row + 1, :] = jnp.zeros((1, LANES), F32)

    for edge, first_x in ((brick == 0, 1), (brick == nb - 1, wx + 2)):

        @pl.when(edge)
        def _():
            fst[first_x] = jnp.zeros((tall, LANES), F32)

    def second_sweep(x):
        y, near = around(fst, x + 2, 1, wy)
        out[x] = 0.1 * y + 0.09 * ext[x + 2, YO : YO + wy, :] + 0.135 * near

    half = wx // 2
    stores = [
        pltpu.make_async_copy(out.at[pl.ds(s * half, half)], res_h.at[pl.ds(s * half, half)], osem.at[s])
        for s in range(2)
    ]
    for s in range(2):
        in_steps(s * half, (s + 1) * half, 8, second_sweep)
        stores[s].start()


    pltpu.make_async_copy(dsend.at[pl.ds(0, 1)], drecv.at[pl.ds(0, 1)], drsem).start()

    pltpu.make_async_copy(drecv, drecv, drsem).wait()
    back = jnp.where(is_id, drecv[...], 0.0).T
    packed = jnp.sum(back.reshape(LANES // CAP, CAP, ndev), axis=0)
    spread = mm(jnp.concatenate([piece for piece in split3(packed)], axis=0), mt[...])
    spread = spread[:CAP] + (spread[CAP : 2 * CAP] + spread[2 * CAP :])
    den[...] = jnp.sum(jnp.where(kmask, spread, 0.0), axis=0, keepdims=True)

    others = pl.ds(1, ndev - 1)
    row_copy(msend.at[others], mrecv.at[others], msem, mrsem, (brick, dom)).wait_send()
    most = pl.ds(CAP, slots - CAP)
    row_copy(send.at[most], recv.at[most], ssem, rsem.at[0], (brick, dom)).wait_send()
    row_copy(drecv.at[others], drecv.at[others], dsem, drsem, (brick, dom)).wait_send()
    for store in stores:
        store.wait()


def body(velocity, adjoint, coupling, jac_weight, owner, local_block, offsets, margin, filtered):
    nb, nd = lax.axis_size("brick"), lax.axis_size("dom")
    ndev = nb * nd
    count = owner.shape[0]
    wx, wy, depth = filtered.shape
    slots = ndev * CAP
    wide = wy + 16
    vmem = pl.BlockSpec(memory_space=pltpu.VMEM)
    hbm = pl.BlockSpec(memory_space=pl.ANY)
    dma = pltpu.SemaphoreType.DMA
    result, density = pl.pallas_call(
        functools.partial(kernel, nb, nd, wx, wy),
        out_shape=(
            jax.ShapeDtypeStruct(filtered.shape, F32),
            jax.ShapeDtypeStruct((1, count), F32),
        ),
        in_specs=[hbm] * 9,
        out_specs=(hbm, vmem),
        scratch_shapes=[
            pltpu.VMEM(coupling.shape, BF16),
            pltpu.VMEM((1, count), F32),
            pltpu.VMEM((1, count), jnp.int32),
            pltpu.VMEM((1, count), jnp.int32),
            pltpu.VMEM(velocity.shape, BF16),
            pltpu.VMEM(adjoint.shape, BF16),
            pltpu.VMEM(offsets.shape, jnp.int32),
            pltpu.VMEM(margin.shape, F32),
            pltpu.VMEM((wx * wy, LANES), F32),
            pltpu.VMEM((ndev, count), BF16),
            pltpu.VMEM((1, count), F32),
            pltpu.VMEM((count, 2 * LANES), BF16),
            pltpu.VMEM((offsets.shape[0], LANES), jnp.int32),
            pltpu.VMEM((LANES // 8, offsets.shape[0], LANES), F32),
            pltpu.VMEM((ndev, LANES), F32),
            pltpu.VMEM((ndev, LANES), F32),
            pltpu.VMEM((slots, LANES), F32),
            pltpu.VMEM((slots, LANES), F32),
            pltpu.VMEM((ndev // 8, LANES), jnp.int32),
            pltpu.SMEM((ndev // 8, LANES), jnp.int32),
            pltpu.VMEM((slots, LANES), F32),
            pltpu.VMEM((slots, LANES), F32),
            pltpu.VMEM((wx * wy, LANES), F32),
            pltpu.VMEM((ndev // 8, LANES), F32),
            pltpu.VMEM((ndev, LANES), F32),
            pltpu.VMEM((wx + 4, wide, LANES), F32),
            pltpu.VMEM((wx + 4, wy + 8, LANES), F32),
            pltpu.VMEM(filtered.shape, F32),
            dma((9,)), dma, dma, dma, dma, dma((nd // 2,)), dma, dma, dma((8,)), dma((8,)), dma((2,)),
        ],
        compiler_params=pltpu.CompilerParams(
            collective_id=0, has_side_effects=True, vmem_limit_bytes=60 * 1024 * 1024
        ),
        name="sensitivity",
    )(
        coupling, jac_weight.reshape(1, count), owner.reshape(1, count),
        local_block.reshape(1, count), velocity, adjoint, offsets, margin,
        filtered.reshape(wx * wy, depth),
    )
    return result, density.reshape(count)


def solution(mesh):
    return jax.shard_map(
        body,
        mesh=mesh,
        in_specs=(
            P(None, None, ("brick", "dom")),
            P(None, None, ("brick", "dom")),
            P(),
            P(("brick", "dom")),
            P(("brick", "dom"), None),
            P(("brick", "dom")),
            P(None, ("brick", "dom")),
            P(None, ("brick", "dom")),
            P("brick", "dom", None),
        ),
        out_specs=(P("brick", "dom", None), P(("brick", "dom"))),
        check_vma=False,
    )
```
